32 devices in a mesh: slab: 2 (over y), gz: 16 (over z, x, core).
Axes of the slice: x: 2, y: 2, z: 4, core: 2. Of those that a mesh axis runs over, the one named last changes fastest.
Arguments:
- eigvecs: bfloat16 [32, 2, 3, 256, 576], P(('slab', 'gz')), parts along dimension 0, may hold values from -6 to 6
- gauge_links: bfloat16 [32, 3, 2, 3, 3, 576], P(('slab', 'gz')), parts along dimension 0, may hold values from -3.5 to 3.5
- momenta: int32 [8, 3], replicated, may hold values from -2 to 2
- directions: int32 [8], replicated, may hold values from 0 to 2, as said below
Outputs:
- elementals: float32 [16, 2, 256, 256], P('slab', None, 'gz'), parts along dimension 0
The draws below stay inside these ranges and needn't reach their ends.
There are 2 independent parts, one for each index of `slab`. The reference program is written for one: setup_inputs(seed, part) draws one part's arguments, and reference() takes and returns one part's arrays. A program takes and returns all parts, laid end to end along the dimension named above; an argument that names none is the same for every part. Nothing has to cross between parts.
Inputs may be any that keep to these rules, and one draw needn't show every extreme that they name: Each of the three directions is named by at least one momentum.
All inputs are finite; a program needn't handle non-finite values.
Results may differ from the reference program's by a relative error of at most 0.0045.
Values may be sent and summed in bfloat16 or wider, within the bound.
No kernel may reach another device: no remote copies, remote signals or barrier semaphores. Data moves between devices by JAX's collectives and lax.ppermute only.
A program may use at most 64 MiB of HBM per device.

```python
import math
import jax
import jax.numpy as jnp
from jax import lax

NX = 96
NY = 96
ZEXT = 96
NV = 256
NP = 8
SITES = 576
NZ = 1
N_GZ = 16


def draw_directions(key, part):
    first_three = jax.random.permutation(jax.random.fold_in(key, 7), 3).astype(jnp.int32)
    others = jax.random.randint(jax.random.fold_in(key, 11), (NP - 3,), 0, 3).astype(jnp.int32)
    combined = jnp.concatenate([first_three, others])
    shuffled = jax.random.permutation(jax.random.fold_in(key, 13), combined)
    return shuffled.astype(jnp.int32)


def plant(result, key, least, largest):
    longest = result.shape.index(max(result.shape))
    spots = []
    for shift in (0, 1):
        where = [jax.random.randint(jax.random.fold_in(key, axis), (), 0, length) for axis, length in enumerate(result.shape)]
        where[longest] = (where[longest] + shift) % result.shape[longest]
        spots.append(tuple(where))
    return result.at[spots[0]].set(least).at[spots[1]].set(largest)


def raised(values, own_key, source, target, parts, factor):
    owner, partner = [(jnp.arange(values.shape[position]) // (values.shape[position] // parts)).reshape([-1 if axis == position else 1 for axis in range(values.ndim)]) for position in (source, target)]
    chosen = jax.random.permutation(own_key, parts)[partner]
    strong = (owner == chosen) | (owner == (partner + parts // 2) % parts)
    return jnp.where(strong, factor * values, values)


def shard_levels(stream_key, shape, shards, least, high):
    level = 1.0
    for dim, shards_of in shards:
        heights = jax.random.uniform(jax.random.fold_in(jax.random.fold_in(stream_key, 6), dim), (shards_of,), jnp.float32, least / len(shards), high / len(shards))
        level = level * jnp.repeat(jnp.exp(heights), shape[dim] // shards_of).reshape((-1,) + (1,) * (len(shape) - 1 - dim))
    return level


def noise(rng, dims, deviation, reach, split=(), kind=jnp.bfloat16):
    level = shard_levels(rng, dims, split, -0.22, 0.18) if split else 1.0
    entries = jax.random.normal(rng, dims, jnp.float32) * deviation * level
    return jnp.minimum(jnp.maximum(entries, -reach), reach).astype(kind)


def noise_with(rng, extent, scale, reach, split, heavy, kind=jnp.bfloat16):
    entries = scale * jax.random.normal(rng, extent, jnp.float32)
    if split:
        entries = entries * shard_levels(rng, extent, split, -0.22, 0.18)
    return jnp.clip(raised(entries, jax.random.fold_in(rng, 3), *heavy), -reach, reach).astype(kind)


def setup_inputs(seed: int = 0, part: int = 0) -> dict:
    streams_of = jax.random.split(jax.random.key(seed), 5)
    own_keys = jax.random.split(jax.random.fold_in(streams_of[4], part), 5)
    eigvecs = noise_with(own_keys[0], (N_GZ, 2, 3, NV, SITES), 1.0, 6.0, ((0, 16),), (0, 3, 16, 2.0))
    gauge_links = noise(own_keys[1], (N_GZ, 3, 2, 3, 3, SITES), 3 ** -0.5, 3.5, ((0, 16),))
    momenta = plant(jax.random.randint(streams_of[2], (NP, 3), -2, 3), jax.random.fold_in(streams_of[2], 1), -2, 2).astype(jnp.int32)
    directions = draw_directions(jax.random.fold_in(streams_of[4], 71), part)
    return dict(eigvecs=eigvecs, gauge_links=gauge_links, momenta=momenta, directions=directions)


two_pi = 2.0 * math.pi


def apply_link(gauge_link, vectors, adjoint):
    real_rows = []
    imag_rows = []
    for i in range(3):
        sum_real = 0.0
        sum_imag = 0.0
        for j in range(3):
            if adjoint:
                link_real = gauge_link[0, j, i, :]
                link_imag = -gauge_link[1, j, i, :]
            else:
                link_real = gauge_link[0, i, j, :]
                link_imag = gauge_link[1, i, j, :]
            link_real = link_real.astype(jnp.float32)[None, :]
            link_imag = link_imag.astype(jnp.float32)[None, :]
            vec_real = vectors[0, j].astype(jnp.float32)
            vec_imag = vectors[1, j].astype(jnp.float32)
            sum_real = sum_real + link_real * vec_real - link_imag * vec_imag
            sum_imag = sum_imag + link_real * vec_imag + link_imag * vec_real
        real_rows.append(sum_real)
        imag_rows.append(sum_imag)
    return jnp.stack([jnp.stack(real_rows), jnp.stack(imag_rows)])


def reference(eigvecs, gauge_links, momenta, directions):
    side_x = NX // 4
    side_y = NY // 4
    z_blocks = N_GZ // 16
    site_count = eigvecs.shape[-1]
    depth = site_count // (side_x * side_y)
    factor = (3.0 * NX * NY * NZ) ** -0.5
    site_index = jnp.arange(site_count).astype(jnp.int32)
    local_z = site_index // (side_x * side_y)
    local_x = (site_index // side_y) % side_x
    local_y = site_index % side_y
    grid_shape = (2, 3, NV, depth, side_x, side_y)
    axis_of = (4, 5, 3)

    def one_block(summed, block):
        bz = block // 16
        bx = (block // 4) % 4
        by = block % 4
        coords = [bx, by, bz]

        def block_at(cx, cy, cz):
            return (((cz % z_blocks) * 16 + (cx % 4) * 4 + cy % 4)).astype(jnp.int32)

        this_vec = lax.dynamic_index_in_dim(eigvecs, block, 0, False)
        this_links = lax.dynamic_index_in_dim(gauge_links, block, 0, False)
        displaced = []
        for d in range(3):
            up_c = list(coords)
            up_c[d] = up_c[d] + 1
            down_c = list(coords)
            down_c[d] = down_c[d] - 1
            up_block = block_at(up_c[0], up_c[1], up_c[2])
            down_block = block_at(down_c[0] + 4, down_c[1] + 4, down_c[2] + z_blocks)
            up_vec = lax.dynamic_index_in_dim(eigvecs, up_block, 0, False)
            down_vec = lax.dynamic_index_in_dim(eigvecs, down_block, 0, False)
            down_links = lax.dynamic_index_in_dim(gauge_links, down_block, 0, False)
            link = this_links[d]
            backward = apply_link(link, this_vec, True).astype(jnp.bfloat16)
            down_back = apply_link(down_links[d], down_vec, True).astype(jnp.bfloat16)
            axis = axis_of[d]
            grid_v = this_vec.reshape(grid_shape)
            grid_up = up_vec.reshape(grid_shape)
            grid_b = backward.reshape(grid_shape)
            grid_down = down_back.reshape(grid_shape)
            length = grid_v.shape[axis]
            ahead = jnp.concatenate([lax.slice_in_dim(grid_v, 1, length, 1, axis),
                                     lax.slice_in_dim(grid_up, 0, 1, 1, axis)], axis).reshape(this_vec.shape)
            behind = jnp.concatenate([lax.slice_in_dim(grid_down, length - 1, length, 1, axis),
                                      lax.slice_in_dim(grid_b, 0, length - 1, 1, axis)], axis).reshape(this_vec.shape)
            forward = apply_link(link, ahead, False)
            displaced.append((0.5 * (forward - behind.astype(jnp.float32))).astype(jnp.bfloat16))
        chosen = jnp.stack(displaced)[directions]
        gx = bx * side_x + local_x
        gy = by * side_y + local_y
        gzz = bz * depth + local_z
        x_mod = jnp.mod(momenta[:, 0:1] * gx[None, :], NX).astype(jnp.float32)
        y_mod = jnp.mod(momenta[:, 1:2] * gy[None, :], NY).astype(jnp.float32)
        z_mod = jnp.mod(momenta[:, 2:3] * gzz[None, :], ZEXT).astype(jnp.float32)
        phase_angle = two_pi * ((x_mod / NX + y_mod / NY) + z_mod / ZEXT)
        cos_part = jnp.cos(phase_angle)[:, None, None, :]
        sin_part = jnp.sin(phase_angle)[:, None, None, :]
        vec_real = this_vec[0].astype(jnp.float32)[None]
        vec_imag = this_vec[1].astype(jnp.float32)[None]
        left_real = (vec_real * cos_part + vec_imag * sin_part).astype(jnp.bfloat16).astype(jnp.float32)
        left_imag = (vec_real * sin_part - vec_imag * cos_part).astype(jnp.bfloat16).astype(jnp.float32)
        disp_real = chosen[:, 0].astype(jnp.float32)
        disp_imag = chosen[:, 1].astype(jnp.float32)
        real_out = jnp.einsum('pcas,pcbs->pab', left_real, disp_real) - jnp.einsum('pcas,pcbs->pab', left_imag, disp_imag)
        imag_out = jnp.einsum('pcas,pcbs->pab', left_real, disp_imag) + jnp.einsum('pcas,pcbs->pab', left_imag, disp_real)
        return summed + jnp.stack([real_out, imag_out], 1), None

    start_sum = jnp.zeros((NP, 2, NV, NV), jnp.float32)
    summed = lax.scan(one_block, start_sum, jnp.arange(N_GZ).astype(jnp.int32))[0]
    return summed * factor
```

```python
import functools
import math

import jax
import jax.numpy as jnp
from jax import lax
from jax.experimental import pallas as pl
from jax.experimental.pallas import tpu as pltpu
from jax.sharding import PartitionSpec as P

NX = 96
NY = 96
ZEXT = 96

LANES = 128
EXTRA = 16
F32 = jnp.float32
BF16 = jnp.bfloat16


def route(count, shift):
    return [(i, (i + shift) % count) for i in range(count)]


def side_route(stride, sign):
    def of(i):
        here = i // stride % 4
        return i + ((here + sign) % 4 - here) * stride

    return of


def faces_kernel(side, v_ref, u_ref, low_x, high_x, low_y, high_y, rows_ref):
    sites = v_ref.shape[-1]
    count = v_ref.shape[2]
    site = lax.broadcasted_iota(jnp.int32, (sites, 4 * LANES), 0)
    lane = lax.broadcasted_iota(jnp.int32, (sites, 4 * LANES), 1)
    face = lane // LANES
    place = lane % LANES
    selectors = []
    for c in range(3):
        k = place - c * side
        wanted = jnp.where(
            face == 0,
            k,
            jnp.where(
                face == 1,
                sites - side + k,
                jnp.where(face == 2, side * k, side * k + side - 1),
            ),
        )
        hit = (site == wanted) & (k >= 0) & (k < side)
        selectors.append(jnp.where(hit, 1.0, 0.0).astype(BF16))
    outs = (low_x, high_x, low_y, high_y)
    for r in range(2):
        total = None
        for c in range(3):
            rows_ref[:count, :] = v_ref[r, c]
            pieces = []
            for d in range(2):
                pieces.append(u_ref[d, r, c].astype(F32))
                pieces.append(u_ref[d, r, :, c, :].astype(F32))
            pieces.append(jnp.zeros((EXTRA - 12, sites), F32))
            rows_ref[count:, :] = jnp.concatenate(pieces, 0).astype(BF16)
            part = jnp.dot(rows_ref[...], selectors[c], preferred_element_type=F32)
            total = part if total is None else total + part
        for f in range(4):
            piece = total[:, f * LANES : (f + 1) * LANES]
            outs[f][:, r * LANES : (r + 1) * LANES] = piece.astype(BF16)


def turn(product, extent):
    return product - extent * jnp.floor(product / extent)


def phase_rows(momenta_ref, gx, gy, gz):
    nx = momenta_ref[:, 0:1].astype(F32)
    ny = momenta_ref[:, 1:2].astype(F32)
    nz = momenta_ref[:, 2:3].astype(F32)
    total = turn(nx * gx, NX) / NX + turn(ny * gy, NY) / NY + turn(nz * gz, ZEXT) / ZEXT
    angle = 2.0 * math.pi * total
    return jnp.cos(angle), jnp.sin(angle)


def main_kernel(
    side,
    z_blocks,
    factor,
    momenta_ref,
    directions_ref,
    v_ref,
    u_ref,
    *rest,
):
    own = rest[0:4]
    halo = rest[4:8]
    rest = rest[8:]
    if z_blocks > 1:
        z_up_ref, z_down_ref, u_down_ref = rest[:3]
        rest = rest[3:]
    keep_ref, send_ref = rest[:2]
    (vp, vs, coef, disp, left, tab, edge_tab, edge_disp, edge_mat, acc) = rest[2:]
    me = lax.axis_index("gz")
    block_z = (me // 16).astype(F32)
    block_x = (me // 4 % 4).astype(F32)
    block_y = (me % 4).astype(F32)
    count = v_ref.shape[2]
    sites = v_ref.shape[3]
    wide = vp.shape[-1]
    tiles = wide // LANES
    np_ = momenta_ref.shape[0]

    lane = lax.broadcasted_iota(jnp.int32, (np_, wide), 1)
    xl = (lane // side).astype(F32)
    yl = (lane % side).astype(F32)
    c_rows, s_rows = phase_rows(
        momenta_ref, block_x * side + xl, block_y * side + yl, block_z
    )
    tab[0] = c_rows
    tab[1] = s_rows
    lane_e = lax.broadcasted_iota(jnp.int32, (np_, LANES), 1)
    k = (lane_e % side).astype(F32)
    x0 = block_x * side
    y0 = block_y * side
    last = float(side - 1)
    for f, (gx, gy) in enumerate(
        ((x0 + 0.0 * k, y0 + k), (x0 + last + 0.0 * k, y0 + k), (x0 + k, y0 + 0.0 * k), (x0 + k, y0 + last + 0.0 * k))
    ):
        c_rows, s_rows = phase_rows(momenta_ref, gx, gy, block_z)
        edge_tab[0, f] = c_rows
        edge_tab[1, f] = s_rows

    for q in range(6):
        vp[q, :, wide - LANES :] = jnp.zeros((count, LANES), BF16)
        vp[q, :, :sites] = v_ref[q // 3, q % 3]

    lane1 = lax.broadcasted_iota(jnp.int32, (1, wide), 1)
    inside = lane1 < sites

    def row(ref, d, r, i, j):
        value = ref[d, r, i, j : j + 1, :].astype(F32)
        return jnp.concatenate([value, jnp.zeros((1, wide - sites), F32)], 1)

    def put(n, value):
        coef[n] = jnp.broadcast_to(value, (8, wide))

    masks = (
        (lane1 < sites - side, (lane1 >= side) & inside),
        (inside & (lane1 % side != side - 1), inside & (lane1 % side != 0)),
    )
    for d in range(2):
        step = (side, 1)[d]
        for i in range(3):
            for j in range(3):
                for r in range(2):
                    u = row(u_ref, d, r, i, j) * 0.5
                    put(((2 * d) * 2 + r) * 9 + 3 * i + j, jnp.where(masks[d][0], u, 0.0))
                    back = pltpu.roll(u, step, 1) * (-1.0 if r == 0 else 1.0)
                    put(((2 * d + 1) * 2 + r) * 9 + 3 * j + i, jnp.where(masks[d][1], back, 0.0))
    if z_blocks > 1:
        for i in range(3):
            for j in range(3):
                for r in range(2):
                    put((8 + r) * 9 + 3 * i + j, row(u_ref, 2, r, i, j) * 0.5)
                    back = row(u_down_ref, 0, r, i, j) * (-0.5 if r == 0 else 0.5)
                    put((10 + r) * 9 + 3 * j + i, back)
    else:
        for i in range(3):
            for j in range(3):
                put(8 * 9 + 3 * i + j, 0.5 * (row(u_ref, 2, 0, i, j) - row(u_ref, 2, 0, j, i)))
                put(9 * 9 + 3 * i + j, 0.5 * (row(u_ref, 2, 1, i, j) + row(u_ref, 2, 1, j, i)))

    shifts = (wide - side, side, wide - 1, 1)

    def shift_rows(n, carry):
        rows = pl.ds(pl.multiple_of(n * 16, 16), 16)
        for q in range(6):
            value = vp[q, rows, :].astype(F32)
            for m, amount in enumerate(shifts):
                vs[m, q, rows, :] = pltpu.roll(value, amount, 1).astype(BF16)
        return carry

    lax.fori_loop(0, count // 16, shift_rows, 0)

    def pair(n, cols):
        c = coef[n, :, cols]
        return jnp.concatenate([c, c], 0)

    def apply(app, vec, cols, sums, skip_diagonal):
        for i in range(3):
            for j in range(3):
                li = pair((2 * app + 1) * 9 + 3 * i + j, cols)
                if not (skip_diagonal and i == j):
                    lr = pair((2 * app) * 9 + 3 * i + j, cols)
                    re = lr * vec[j]
                    im = lr * vec[3 + j]
                    sums[i] = re if sums[i] is None else sums[i] + re
                    sums[3 + i] = im if sums[3 + i] is None else sums[3 + i] + im
                re = li * vec[3 + j]
                im = li * vec[j]
                sums[i] = -re if sums[i] is None else sums[i] - re
                sums[3 + i] = im if sums[3 + i] is None else sums[3 + i] + im
        return sums

    def displace(n, carry):
        rows = pl.ds(pl.multiple_of(n * 16, 16), 16)

        def one_tile(t, inner):
            cols = pl.ds(pl.multiple_of(t * LANES, LANES), LANES)
            for d in range(3):
                sums = [None] * 6
                if d < 2:
                    for side_of in range(2):
                        vec = [vs[2 * d + side_of, q, rows, cols].astype(F32) for q in range(6)]
                        sums = apply(2 * d + side_of, vec, cols, sums, False)
                elif z_blocks > 1:
                    pass
                else:
                    vec = [vp[q, rows, cols].astype(F32) for q in range(6)]
                    sums = apply(4, vec, cols, sums, True)
                if d < 2 or z_blocks == 1:
                    for q in range(6):
                        at = pl.ds(pl.multiple_of((q % 3) * wide + t * LANES, LANES), LANES)
                        disp[d, q // 3, rows, at] = sums[q].astype(BF16)
            return inner

        return lax.fori_loop(0, tiles, one_tile, carry)

    lax.fori_loop(0, count // 16, displace, 0)

    if z_blocks > 1:
        for q in range(6):
            for m, ref in enumerate((z_up_ref, z_down_ref)):
                vs[m, q, :, wide - LANES :] = jnp.zeros((count, LANES), BF16)
                vs[m, q, :, :sites] = ref[q // 3, q % 3]

        def displace_z(n, carry):
            rows = pl.ds(pl.multiple_of(n * 16, 16), 16)

            def one_tile(t, inner):
                cols = pl.ds(pl.multiple_of(t * LANES, LANES), LANES)
                sums = [None] * 6
                for m in range(2):
                    vec = [vs[m, q, rows, cols].astype(F32) for q in range(6)]
                    sums = apply(4 + m, vec, cols, sums, False)
                for q in range(6):
                    at = pl.ds(pl.multiple_of((q % 3) * wide + t * LANES, LANES), LANES)
                    disp[2, q // 3, rows, at] = sums[q].astype(BF16)
                return inner

            return lax.fori_loop(0, tiles, one_tile, carry)

        lax.fori_loop(0, count // 16, displace_z, 0)

    diagonal_row = lax.broadcasted_iota(jnp.int32, (side, LANES), 0)
    diagonal_lane = lax.broadcasted_iota(jnp.int32, (side, LANES), 1)
    hit = (diagonal_lane % side == diagonal_row) & (diagonal_lane < 3 * side)
    for d in range(2):
        for f in range(2):
            source = halo[2 * d + f]
            links_of = own[2 * d + 1] if f == 0 else halo[2 * d + 1]
            first = count + 6 * d + (0 if f == 0 else 3)
            tile = links_of[count:, :].astype(F32)
            for form in range(2):
                edge_mat[...] = jnp.zeros(edge_mat.shape, BF16)
                for r in range(2):
                    for j in range(3):
                        at = first - count + j
                        ur = tile[at : at + 1, :LANES]
                        ui = tile[at : at + 1, LANES:]
                        if f == 0:
                            re, im = (ur, ui) if r == 0 else (-ui, ur)
                            scale = 0.5
                        else:
                            re, im = (ur, -ui) if r == 0 else (ui, ur)
                            scale = -0.5
                        first_half, second_half = (re, -im) if form == 0 else (im, re)
                        for h, value in enumerate((first_half, second_half)):
                            block = jnp.where(hit, value * scale, 0.0).astype(BF16)
                            edge_mat[
                                r * LANES + j * side : r * LANES + (j + 1) * side,
                                h * LANES : (h + 1) * LANES,
                            ] = block
                edge_disp[2 * d + f, form] = jnp.dot(
                    source[:count, :], edge_mat[...], preferred_element_type=F32
                ).astype(BF16)

    def dot_t(a, b):
        return lax.dot_general(a, b, (((1,), (1,)), ((), ())), preferred_element_type=F32)

    mine = me % 2
    for p in range(np_):
        d = directions_ref[p]

        def make_left(n, carry):
            rows = pl.ds(pl.multiple_of(n * 16, 16), 16)
            for t in range(tiles):
                cols = slice(t * LANES, (t + 1) * LANES)
                c = jnp.broadcast_to(tab[0, p : p + 1, cols], (16, LANES))
                s = jnp.broadcast_to(tab[1, p : p + 1, cols], (16, LANES))
                for q in range(3):
                    vr = vp[q, rows, cols].astype(F32)
                    vi = vp[3 + q, rows, cols].astype(F32)
                    at = slice(q * wide + t * LANES, q * wide + (t + 1) * LANES)
                    left[0, rows, at] = (vr * c + vi * s).astype(BF16)
                    left[1, rows, at] = (vr * s - vi * c).astype(BF16)
            return carry

        lax.fori_loop(0, count // 16, make_left, 0)
        lr = left[0]
        li = left[1]
        out_re = dot_t(lr, disp[d, 0]) - dot_t(li, disp[d, 1])
        out_im = dot_t(lr, disp[d, 1]) + dot_t(li, disp[d, 0])
        acc[0] = (out_re * factor).reshape(acc.shape[1:])
        acc[1] = (out_im * factor).reshape(acc.shape[1:])

        for axis in range(2):

            @pl.when(d == axis)
            def _():
                for f in range(2):
                    own_face = 2 * axis + 1 - f
                    c = edge_tab[0, own_face, p : p + 1, :]
                    s = edge_tab[1, own_face, p : p + 1, :]
                    tr = own[own_face][:count, :LANES].astype(F32)
                    ti = own[own_face][:count, LANES:].astype(F32)
                    el = jnp.concatenate([tr * c + ti * s, tr * s - ti * c], 1).astype(BF16)
                    for form in range(2):
                        extra = dot_t(el, edge_disp[2 * axis + f, form]) * factor
                        acc[form] = acc[form] + extra.reshape(acc.shape[1:])

        for form in range(2):
            keep_ref[p, form] = acc[form, :, mine]
            send_ref[p, form] = acc[form, :, 1 - mine].astype(BF16)


def halve(keep, send, order, me):
    count = lax.axis_size("gz")
    bits = sorted(order, reverse=True)
    bits.remove(order[0])
    for n, bit in enumerate(order):
        got = lax.ppermute(send, "gz", [(i, i ^ bit) for i in range(count)])
        total = keep + got.astype(F32)
        if n + 1 == len(order):
            return total
        following = order[n + 1]
        axis = bits.index(following)
        bits.remove(following)
        lead = total.shape[:2]
        rows = total.shape[2]
        inner = 2 ** (len(bits) - axis)
        outer = 2**axis
        tail = rows // (outer * 2 * inner)
        split = total.reshape(lead + (outer, 2, inner * tail, total.shape[-1]))
        mine = me // following % 2
        keep = lax.dynamic_index_in_dim(split, mine, 3, False)
        send = lax.dynamic_index_in_dim(split, 1 - mine, 3, False).astype(BF16)
        keep = keep.reshape(lead + (rows // 2, total.shape[-1]))
        send = send.reshape(lead + (rows // 2, total.shape[-1]))


def body(eigvecs, gauge_links, momenta, directions):
    device_count = lax.axis_size("gz")
    me = lax.axis_index("gz")
    v = eigvecs[0]
    u = gauge_links[0]
    side = NX // 4
    count, sites = v.shape[2:]
    z_blocks = device_count // 16
    if sites != side * (NY // 4) or device_count & (device_count - 1) or count % (2 * device_count) and count % device_count:
        raise ValueError("unsupported block")
    np_ = momenta.shape[0]
    factor = (3.0 * NX * NY * z_blocks) ** (-0.5)
    wide = -(-sites // LANES) * LANES
    vmem = pl.BlockSpec(memory_space=pltpu.VMEM)
    smem = pl.BlockSpec(memory_space=pltpu.SMEM)
    pack = jax.ShapeDtypeStruct((count + EXTRA, 2 * LANES), BF16)
    packs = pl.pallas_call(
        functools.partial(faces_kernel, side),
        out_shape=[pack] * 4,
        in_specs=[vmem] * 2,
        out_specs=[vmem] * 4,
        scratch_shapes=[pltpu.VMEM((count + EXTRA, sites), BF16)],
        name="faces",
    )(v, u)
    low_x, high_x, low_y, high_y = packs

    def sent(face, stride, sign):
        of = side_route(stride, sign)
        return lax.ppermute(face, "gz", [(i, of(i)) for i in range(device_count)])

    halos = [
        sent(low_x, 4, -1),
        sent(high_x, 4, 1),
        sent(low_y, 1, -1),
        sent(high_y, 1, 1),
    ]
    operands = [momenta, directions, v, u, *packs, *halos]
    specs = [vmem, smem] + [vmem] * 10
    if z_blocks > 1:
        operands += [
            lax.ppermute(v, "gz", route(device_count, -16)),
            lax.ppermute(v, "gz", route(device_count, 16)),
            lax.ppermute(u[2:3], "gz", route(device_count, 16)),
        ]
        specs += [vmem] * 3
    half = count // 2
    per = count // device_count
    applications = 6 if z_blocks > 1 else 5
    keep, send = pl.pallas_call(
        functools.partial(main_kernel, side, z_blocks, factor),
        out_shape=[
            jax.ShapeDtypeStruct((np_, 2, device_count // 2, per, count), F32),
            jax.ShapeDtypeStruct((np_, 2, device_count // 2, per, count), BF16),
        ],
        in_specs=specs,
        out_specs=[vmem] * 2,
        scratch_shapes=[
            pltpu.VMEM((6, count, wide), BF16),
            pltpu.VMEM((4, 6, count, wide), BF16),
            pltpu.VMEM((applications * 18, 8, wide), F32),
            pltpu.VMEM((3, 2, count, 3 * wide), BF16),
            pltpu.VMEM((2, count, 3 * wide), BF16),
            pltpu.VMEM((2, np_, wide), F32),
            pltpu.VMEM((2, 4, np_, LANES), F32),
            pltpu.VMEM((4, 2, count, 2 * LANES), BF16),
            pltpu.VMEM((2 * LANES, 2 * LANES), BF16),
            pltpu.VMEM((2, device_count // 2, 2, per, count), F32),
        ],
        name="products",
    )(*operands)
    keep = keep.reshape(np_, 2, half, count)
    send = send.reshape(np_, 2, half, count)
    order = [2**n for n in range(device_count.bit_length() - 1)]
    other = [order[0], order[2], order[1]] + order[3:]
    cut = np_ // 2
    first = halve(keep[:cut], send[:cut], order, me)
    second = halve(keep[cut:], send[cut:], other, me)
    return jnp.concatenate([first, second], 0)


def solution(mesh):
    return jax.shard_map(
        body,
        mesh=mesh,
        in_specs=(
            P(("slab", "gz"), None, None, None, None),
            P(("slab", "gz"), None, None, None, None, None),
            P(),
            P(),
        ),
        out_specs=P("slab", None, "gz", None),
        check_vma=False,
    )
```

```python
import functools
import math

import jax
import jax.numpy as jnp
from jax import lax
from jax.experimental import pallas as pl
from jax.experimental.pallas import tpu as pltpu
from jax.sharding import PartitionSpec as P

NX = 96
NY = 96
ZEXT = 96

LANES = 128
EXTRA = 32
VMEM_LIMIT = 30 * 2**20
F32 = jnp.float32
BF16 = jnp.bfloat16


def route(count, shift):
    return [(i, (i + shift) % count) for i in range(count)]


def side_route(stride, sign):
    def of(i):
        here = i // stride % 4
        return i + ((here + sign) % 4 - here) * stride

    return of


def wide_row(rows, wide):
    pad = jnp.zeros((rows.shape[0], wide - rows.shape[1]), F32)
    return jnp.concatenate([rows, pad], 1)


def link_rows(ref, d):
    return jnp.concatenate([ref[d, i, j].astype(F32) for i in range(3) for j in range(3)], 0)


def faces_kernel(side, place, v_ref, u_ref, low_x, high_x, low_y, high_y, near_ref, v32):
    sites = v_ref.shape[2]
    last = side - 1
    for q in range(6):
        rows = pl.ds(q * side, side)
        low_x[rows, :] = v_ref[q // 3, q % 3, :side, :]
        high_x[rows, :] = v_ref[q // 3, q % 3, sites - side :, :]
        for h in range(v32.shape[0]):
            at = slice(h * LANES, (h + 1) * LANES)
            v32[h] = v_ref[q // 3, q % 3, :, at].astype(F32)
            low_y[rows, at] = v32[h, pl.ds(0, side, stride=side), :].astype(BF16)
            high_y[rows, at] = v32[h, pl.ds(last, side, stride=side), :].astype(BF16)
    site = lax.broadcasted_iota(jnp.int32, (sites, LANES), 0)
    lane = lax.broadcasted_iota(jnp.int32, (sites, LANES), 1)
    k = lane - place
    wanted_y = jnp.where(k < side, k, k - side) * side + last
    wanted = jnp.where(lane < side, sites - side + lane, wanted_y)
    hit = (site == wanted) & ((lane < side) | ((k >= 0) & (k < 2 * side)))
    pick = jnp.where(hit, 1.0, 0.0).astype(BF16)
    rest = jnp.zeros((EXTRA - 18, LANES), F32)
    for d, out in enumerate((high_x, high_y)):
        rows = link_rows(u_ref, d).astype(BF16)
        taken = jnp.dot(rows, pick, preferred_element_type=F32)
        taken = jnp.concatenate([taken, rest], 0).astype(BF16)
        out[6 * side :, :] = jnp.concatenate([taken, taken], 1)
        if d == 1:
            near_ref[...] = taken


def turn(product, extent):
    return product - extent * jnp.floor(product / extent)


def phase_rows(momenta_ref, gx, gy, gz):
    nx = momenta_ref[:, 0:1].astype(F32)
    ny = momenta_ref[:, 1:2].astype(F32)
    nz = momenta_ref[:, 2:3].astype(F32)
    total = turn(nx * gx, NX) / NX + turn(ny * gy, NY) / NY + turn(nz * gz, ZEXT) / ZEXT
    angle = 2.0 * math.pi * total
    return jnp.cos(angle), jnp.sin(angle)


def put(coef, app, i, j, re, im):
    for n, value in enumerate((re, im, re + im)):
        coef[app * 27 + n * 9 + 3 * i + j] = jnp.broadcast_to(value, coef.shape[1:])


def place_of(q, t, tiles):
    inner = tiles - 2
    if 0 < t < tiles - 1:
        return q * inner + t - 1
    return 3 * inner + q * 2 + (t > 0)


def displace_tile(apps, skip_diagonal=False):
    def pair(links, app, n, i, j, cols):
        c = links[app * 27 + n * 9 + 3 * i + j, :, cols]
        return jnp.concatenate([c, c], 0)

    def add(a, b):
        return b if a is None else a + b

    joined = [[vec[j] + vec[3 + j] for j in range(3)] for _, _, _, vec in apps]
    out = [None] * 6
    for i in range(3):
        p1 = p2 = p3 = None
        for (links, app, cols, vec), both in zip(apps, joined):
            for j in range(3):
                if not (skip_diagonal and i == j):
                    p1 = add(p1, pair(links, app, 0, i, j, cols) * vec[j])
                p2 = add(p2, pair(links, app, 1, i, j, cols) * vec[3 + j])
                p3 = add(p3, pair(links, app, 2, i, j, cols) * both[j])
        out[i] = p1 - p2
        out[3 + i] = p3 - p1 - p2
    return out


def store_tile(ref, d, n, q_places, count, values):
    for q in range(6):
        rows = pl.ds(pl.multiple_of((q // 3) * count + n * 16, 16), 16)
        at = slice(q_places[q % 3] * LANES, (q_places[q % 3] + 1) * LANES)
        ref[d, rows, at] = values[q].astype(BF16)


def interior_kernel(side, z_blocks, momenta_ref, v_ref, u_ref, low_y, high_y, *rest):
    if z_blocks > 1:
        z_up_ref, z_down_ref, u_down_ref = rest[:3]
        rest = rest[3:]
        vz = rest[3]
        rest = rest[:3] + rest[4:]
    vp, tab, coef, inner_ref, vs = rest[0], rest[1], rest[2], rest[3], rest[4]
    me = lax.axis_index("gz")
    block_z = (me // 16).astype(F32)
    block_x = (me // 4 % 4).astype(F32)
    block_y = (me % 4).astype(F32)
    sites = v_ref.shape[2]
    count = v_ref.shape[3]
    wide = vp.shape[-1]
    tiles = wide // LANES
    np_ = momenta_ref.shape[0]

    lane = lax.broadcasted_iota(jnp.int32, (np_, wide), 1)
    behind = lane - sites
    on_face = behind >= 0
    xl = jnp.where(on_face, behind % side, lane // side).astype(F32)
    yl = jnp.where(on_face, jnp.where(behind < side, side - 1, 0), lane % side).astype(F32)
    c_rows, s_rows = phase_rows(momenta_ref, block_x * side + xl, block_y * side + yl, block_z)
    tab[0] = c_rows
    tab[1] = s_rows

    for q in range(6):
        at = slice(q * side, (q + 1) * side)
        pieces = [
            v_ref[q // 3, q % 3].astype(F32),
            high_y[at, :].astype(F32),
            low_y[at, :].astype(F32),
            jnp.zeros((wide - sites - 2 * side, count), F32),
        ]
        vp[q] = jnp.concatenate(pieces, 0).T.astype(BF16)

    lane1 = lax.broadcasted_iota(jnp.int32, (1, wide), 1)
    inside = lane1 < sites
    masks = (
        (inside, inside & (lane1 >= side)),
        (inside & (lane1 % side != side - 1), inside & (lane1 % side != 0)),
    )
    for d in range(2):
        rows = wide_row(link_rows(u_ref, d) * 0.5, wide)
        ahead = jnp.where(masks[d][0], rows, 0.0)
        back = jnp.where(masks[d][1], pltpu.roll(rows, (side, 1)[d], 1), 0.0)
        for i in range(3):
            for j in range(3):
                n = (3 * i + j) * 2
                put(coef, 2 * d, i, j, ahead[n : n + 1], ahead[n + 1 : n + 2])
                put(coef, 2 * d + 1, j, i, -back[n : n + 1], back[n + 1 : n + 2])
    rows = wide_row(link_rows(u_ref, 2) * 0.5, wide)
    if z_blocks > 1:
        back = wide_row(link_rows(u_down_ref, 0) * 0.5, wide)
    for i in range(3):
        for j in range(3):
            n = (3 * i + j) * 2
            m = (3 * j + i) * 2
            if z_blocks > 1:
                put(coef, 4, i, j, rows[n : n + 1], rows[n + 1 : n + 2])
                put(coef, 5, j, i, -back[n : n + 1], back[n + 1 : n + 2])
            else:
                put(coef, 4, i, j, rows[n : n + 1] - rows[m : m + 1], rows[n + 1 : n + 2] + rows[m + 1 : m + 2])
    if z_blocks > 1:
        for q in range(6):
            for m, ref in enumerate((z_up_ref, z_down_ref)):
                value = ref[q // 3, q % 3].astype(F32)
                value = jnp.concatenate([value, jnp.zeros((wide - sites, count), F32)], 0)
                vz[m, q] = value.T.astype(BF16)

    shifts = (wide - side, side, wide - 1, 1)

    def displace(n, carry):
        rows = pl.ds(pl.multiple_of(n * 16, 16), 16)
        for q in range(6):
            value = vp[q, rows, :].astype(F32)
            for m, amount in enumerate(shifts):
                vs[m, q] = pltpu.roll(value, amount, 1)
        for t in range(1, tiles - 1):
            cols = slice(t * LANES, (t + 1) * LANES)
            spots = [place_of(q, t, tiles) for q in range(3)]
            for d in range(2):
                apps = [(coef, 2 * d + m, cols, [vs[2 * d + m, q, :, cols] for q in range(6)]) for m in range(2)]
                store_tile(inner_ref, d, n, spots, count, displace_tile(apps))
            if z_blocks == 1:
                vec = [vp[q, rows, cols].astype(F32) for q in range(6)]
                values = displace_tile([(coef, 4, cols, vec)], True)
            else:
                apps = [(coef, 4 + m, cols, [vz[m, q, rows, cols].astype(F32) for q in range(6)]) for m in range(2)]
                values = displace_tile(apps)
            store_tile(inner_ref, 2, n, spots, count, values)
        return carry

    lax.fori_loop(0, count // 16, displace, 0)


def border(side, sites, vp, vz, coef, near_ref, halo, outer, halo_t, side_coef):
    up_x, down_x, up_y, down_y = halo
    count = vp.shape[1]
    wide = vp.shape[-1]
    tiles = wide // LANES
    tail = sites - (tiles - 1) * LANES
    first = slice(0, LANES)
    final = slice((tiles - 1) * LANES, wide)
    for q in range(6):
        at = slice(q * side, (q + 1) * side)
        pieces = [
            down_x[at, :].astype(F32),
            jnp.zeros((tail - 2 * side, count), F32),
            up_x[at, :].astype(F32),
            up_y[at, :].astype(F32),
            down_y[at, :].astype(F32),
            jnp.zeros((LANES - tail - 2 * side, count), F32),
        ]
        halo_t[q] = jnp.concatenate(pieces, 0).T.astype(BF16)
    lane = lax.broadcasted_iota(jnp.int32, (1, LANES), 1)
    rows_x = down_x[6 * side :, :LANES].astype(F32) * 0.5
    rows_y = down_y[6 * side :, :LANES].astype(F32) * 0.5
    near = near_ref[...].astype(F32) * 0.5
    up_lanes = (lane >= tail) & (lane < tail + side)
    down_lanes = (lane >= tail + side) & (lane < tail + 2 * side)
    for i in range(3):
        for j in range(3):
            n = (3 * i + j) * 2
            m = (3 * j + i) * 2
            re = jnp.where(lane < side, -rows_x[m : m + 1], coef[27 + 3 * i + j, 0:1, first])
            im = jnp.where(lane < side, rows_x[m + 1 : m + 2], coef[27 + 9 + 3 * i + j, 0:1, first])
            put(side_coef, 0, i, j, re, im)
            re = jnp.where(up_lanes, near[n : n + 1], jnp.where(down_lanes, -rows_y[m : m + 1], 0.0))
            im = jnp.where(up_lanes, near[n + 1 : n + 2], jnp.where(down_lanes, rows_y[m + 1 : m + 2], 0.0))
            put(side_coef, 1, i, j, re, im)

    lane16 = lax.broadcasted_iota(jnp.int32, (16, LANES), 1)
    alone = slice(0, LANES)
    base = 3 * (tiles - 2)

    def one(n, carry):
        rows = pl.ds(pl.multiple_of(n * 16, 16), 16)
        got = [halo_t[q, rows, :].astype(F32) for q in range(6)]
        start = [vp[q, rows, 0 : 2 * LANES].astype(F32) for q in range(6)]
        spots = [place_of(q, 0, tiles) - base for q in range(3)]
        ahead = [pltpu.roll(a, 2 * LANES - side, 1)[:, :LANES] for a in start]
        behind = [jnp.where(lane16 < side, g, pltpu.roll(a[:, :LANES], side, 1)) for a, g in zip(start, got)]
        store_tile(outer, 0, n, spots, count, displace_tile([(coef, 0, first, ahead), (side_coef, 0, alone, behind)]))
        ahead = [pltpu.roll(a, 2 * LANES - 1, 1)[:, :LANES] for a in start]
        behind = [pltpu.roll(a[:, :LANES], 1, 1) for a in start]
        store_tile(outer, 1, n, spots, count, displace_tile([(coef, 2, first, ahead), (coef, 3, first, behind)]))
        if vz is None:
            values = displace_tile([(coef, 4, first, [a[:, :LANES] for a in start])], True)
        else:
            values = displace_tile([(coef, 4 + m, first, [vz[m, q, rows, first].astype(F32) for q in range(6)]) for m in range(2)])
        store_tile(outer, 2, n, spots, count, values)

        end = [vp[q, rows, wide - 2 * LANES : wide].astype(F32) for q in range(6)]
        spots = [place_of(q, tiles - 1, tiles) - base for q in range(3)]
        ahead = [jnp.where(lane16 >= tail - side, g, pltpu.roll(a[:, LANES:], LANES - side, 1)) for a, g in zip(end, got)]
        behind = [pltpu.roll(a, side, 1)[:, LANES:] for a in end]
        store_tile(outer, 0, n, spots, count, displace_tile([(coef, 0, final, ahead), (coef, 1, final, behind)]))
        ahead = [pltpu.roll(a[:, LANES:], LANES - 1, 1) for a in end]
        behind = [pltpu.roll(a, 1, 1)[:, LANES:] for a in end]
        apps = [(coef, 2, final, ahead), (coef, 3, final, behind), (side_coef, 1, alone, got)]
        store_tile(outer, 1, n, spots, count, displace_tile(apps))
        if vz is None:
            values = displace_tile([(coef, 4, final, [a[:, LANES:] for a in end])], True)
        else:
            values = displace_tile([(coef, 4 + m, final, [vz[m, q, rows, final].astype(F32) for q in range(6)]) for m in range(2)])
        store_tile(outer, 2, n, spots, count, values)
        return carry

    lax.fori_loop(0, count // 16, one, 0)


def products_kernel(side, sites, z_blocks, factor, start, stop, with_border, directions_ref, vp, tab, inner_ref, *rest):
    me = lax.axis_index("gz")
    if with_border:
        coef, near_ref = rest[:2]
        halo = rest[2:6]
        rest = rest[6:]
        vz = None
        if z_blocks > 1:
            vz = rest[0]
            rest = rest[1:]
        keep_ref, send_ref, outer = rest[:3]
        left, acc, halo_t, side_coef = rest[3:]
        border(side, sites, vp, vz, coef, near_ref, halo, outer, halo_t, side_coef)
    else:
        outer = rest[0]
        keep_ref, send_ref, left, acc = rest[1:]
    count = vp.shape[1]
    tiles = vp.shape[2] // LANES
    cut = 3 * (tiles - 2) * LANES
    mine = me % 2

    def dot_t(a, b):
        return lax.dot_general(a, b, (((1,), (1,)), ((), ())), preferred_element_type=F32)

    for p in range(start, stop):
        d = directions_ref[p]

        def make_left(n, carry):
            rows = pl.ds(pl.multiple_of(n * 16, 16), 16)
            lower = pl.ds(pl.multiple_of(count + n * 16, 16), 16)
            for t in range(tiles):
                cols = slice(t * LANES, (t + 1) * LANES)
                c = jnp.broadcast_to(tab[0, p : p + 1, cols], (16, LANES))
                s = jnp.broadcast_to(tab[1, p : p + 1, cols], (16, LANES))
                for q in range(3):
                    vr = vp[q, rows, cols].astype(F32)
                    vi = vp[3 + q, rows, cols].astype(F32)
                    spot = place_of(q, t, tiles)
                    at = slice(spot * LANES, (spot + 1) * LANES)
                    left[rows, at] = (vr * c + vi * s).astype(BF16)
                    left[lower, at] = (vr * s - vi * c).astype(BF16)
            return carry

        lax.fori_loop(0, count // 16, make_left, 0)
        both = dot_t(left[:, :cut], inner_ref[d]) + dot_t(left[:, cut:], outer[d])
        out_re = both[:count, :count] - both[count:, count:]
        out_im = both[:count, count:] + both[count:, :count]
        acc[0] = (out_re * factor).reshape(acc.shape[1:])
        acc[1] = (out_im * factor).reshape(acc.shape[1:])
        for form in range(2):
            keep_ref[p - start, form] = acc[form, :, mine]
            send_ref[p - start, form] = acc[form, :, 1 - mine].astype(BF16)


def halve(keep, send, order, me):
    count = lax.axis_size("gz")
    bits = sorted(order, reverse=True)
    bits.remove(order[0])
    for n, bit in enumerate(order):
        got = lax.ppermute(send, "gz", [(i, i ^ bit) for i in range(count)])
        total = keep + got.astype(F32)
        if n + 1 == len(order):
            return total
        following = order[n + 1]
        axis = bits.index(following)
        bits.remove(following)
        lead = total.shape[:2]
        rows = total.shape[2]
        inner = 2 ** (len(bits) - axis)
        outer = 2**axis
        tail = rows // (outer * 2 * inner)
        split = total.reshape(lead + (outer, 2, inner * tail, total.shape[-1]))
        mine = me // following % 2
        keep = lax.dynamic_index_in_dim(split, mine, 3, False)
        send = lax.dynamic_index_in_dim(split, 1 - mine, 3, False).astype(BF16)
        keep = keep.reshape(lead + (rows // 2, total.shape[-1]))
        send = send.reshape(lead + (rows // 2, total.shape[-1]))


def body(eigvecs, gauge_links, momenta, directions):
    device_count = lax.axis_size("gz")
    me = lax.axis_index("gz")
    v = jnp.swapaxes(eigvecs[0], 2, 3)
    u = jnp.transpose(gauge_links[0], (0, 2, 3, 1, 4))
    side = NX // 4
    sites, count = v.shape[2:]
    z_blocks = device_count // 16
    wide = -(-sites // LANES) * LANES
    tiles = wide // LANES
    tail = sites - wide + LANES
    if sites != side * (NY // 4) or device_count & (device_count - 1) or count % device_count:
        raise ValueError("unsupported block")
    if tiles < 3 or tail < 2 * side or tail + 2 * side > LANES:
        raise ValueError("unsupported sites")
    np_ = momenta.shape[0]
    factor = (3.0 * NX * NY * z_blocks) ** (-0.5)
    vmem = pl.BlockSpec(memory_space=pltpu.VMEM)
    smem = pl.BlockSpec(memory_space=pltpu.SMEM)
    params = pltpu.CompilerParams(vmem_limit_bytes=VMEM_LIMIT)
    low = jax.ShapeDtypeStruct((6 * side, count), BF16)
    high = jax.ShapeDtypeStruct((6 * side + EXTRA, count), BF16)
    low_x, high_x, low_y, high_y, near = pl.pallas_call(
        functools.partial(faces_kernel, side, tail),
        out_shape=[low, high, low, high, jax.ShapeDtypeStruct((EXTRA, LANES), BF16)],
        in_specs=[vmem] * 2,
        out_specs=[vmem] * 5,
        scratch_shapes=[pltpu.VMEM((count // LANES, sites, LANES), F32)],
        compiler_params=params,
        name="faces",
    )(v, u)

    def sent(face, stride, sign):
        of = side_route(stride, sign)
        return lax.ppermute(face, "gz", [(i, of(i)) for i in range(device_count)])

    halos = [
        sent(low_x, 4, -1),
        sent(high_x, 4, 1),
        sent(low_y, 1, -1),
        sent(high_y, 1, 1),
    ]
    applications = 6 if z_blocks > 1 else 5
    operands = [momenta, v, u, low_y, high_y]
    moved = jax.ShapeDtypeStruct((6, count, wide), BF16)
    shapes = [
        moved,
        jax.ShapeDtypeStruct((2, np_, wide), F32),
        jax.ShapeDtypeStruct((applications * 27, 8, wide), F32),
    ]
    if z_blocks > 1:
        operands += [
            lax.ppermute(v, "gz", route(device_count, -16)),
            lax.ppermute(v, "gz", route(device_count, 16)),
            lax.ppermute(u[2:3], "gz", route(device_count, 16)),
        ]
        shapes.append(jax.ShapeDtypeStruct((2, 6, count, wide), BF16))
    shapes.append(jax.ShapeDtypeStruct((3, 2 * count, 3 * (tiles - 2) * LANES), BF16))
    results = pl.pallas_call(
        functools.partial(interior_kernel, side, z_blocks),
        out_shape=shapes,
        in_specs=[vmem] * len(operands),
        out_specs=[vmem] * len(shapes),
        scratch_shapes=[pltpu.VMEM((4, 6, 16, wide), F32)],
        compiler_params=params,
        name="interior",
    )(*operands)
    vp, tab, coef, inner = results[0], results[1], results[2], results[-1]
    vz = list(results[3:-1])
    half = count // 2
    per = count // device_count
    lead = (device_count // 2, per, count)

    def products(start, stop, extra):
        with_border = len(extra) > 1
        operands = [directions, vp, tab, inner, *extra]
        shapes = [
            jax.ShapeDtypeStruct((stop - start, 2) + lead, F32),
            jax.ShapeDtypeStruct((stop - start, 2) + lead, BF16),
        ]
        scratch = [
            pltpu.VMEM((2 * count, 3 * wide), BF16),
            pltpu.VMEM((2, device_count // 2, 2, per, count), F32),
        ]
        if with_border:
            shapes.append(jax.ShapeDtypeStruct((3, 2 * count, 6 * LANES), BF16))
            scratch += [
                pltpu.VMEM((6, count, LANES), BF16),
                pltpu.VMEM((2 * 27, 8, LANES), F32),
            ]
        results = pl.pallas_call(
            functools.partial(products_kernel, side, sites, z_blocks, factor, start, stop, with_border),
            out_shape=shapes,
            in_specs=[smem] + [vmem] * (len(operands) - 1),
            out_specs=[vmem] * len(shapes),
            scratch_shapes=scratch,
            compiler_params=params,
            name=f"products_{start}",
        )(*operands)
        flat = (stop - start, 2, half, count)
        return results[0].reshape(flat), results[1].reshape(flat), results[2:]

    order = [2**n for n in range(device_count.bit_length() - 1)]
    other = [order[0], order[2], order[1]] + order[3:]
    cut = np_ // 2
    keep, send, (outer,) = products(0, cut, [coef, near, *halos, *vz])
    first = halve(keep, send, order, me)
    keep, send, _ = products(cut, np_, [outer])
    second = halve(keep, send, other, me)
    return jnp.concatenate([first, second], 0)


def solution(mesh):
    return jax.shard_map(
        body,
        mesh=mesh,
        in_specs=(
            P(("slab", "gz"), None, None, None, None),
            P(("slab", "gz"), None, None, None, None, None),
            P(),
            P(),
        ),
        out_specs=P("slab", None, "gz", None),
        check_vma=False,
    )
```

```python
import functools
import math

import jax
import jax.numpy as jnp
from jax import lax
from jax.experimental import pallas as pl
from jax.experimental.pallas import tpu as pltpu
from jax.sharding import PartitionSpec as P

NX = 96
NY = 96
ZEXT = 96

LANES = 128
VMEM_LIMIT = 30 * 2**20
CUTS = (5, 6)
FACES_LIMIT = 30 * 2**20
F32 = jnp.float32
BF16 = jnp.bfloat16


def route(count, shift):
    return [(i, (i + shift) % count) for i in range(count)]


def side_route(stride, sign):
    def of(i):
        here = i // stride % 4
        return i + ((here + sign) % 4 - here) * stride

    return of


def wide_row(rows, wide):
    pad = jnp.zeros((rows.shape[0], wide - rows.shape[1]), F32)
    return jnp.concatenate([rows, pad], 1)


def link_rows(ref, d):
    return jnp.concatenate([ref[d, i, j].astype(F32) for i in range(3) for j in range(3)], 0)


def faces_kernel(
    side, momenta_in, v_in, u_in, momenta_ref, v_ref, u_ref, low_x, low_y, high_y, v32, v_sems, sems
):
    copies = [
        pltpu.make_async_copy(v_in.at[q // 3, q % 3], v_ref.at[q // 3, q % 3], v_sems.at[q]) for q in range(6)
    ]
    copies.append(pltpu.make_async_copy(u_in, u_ref, sems.at[0]))
    copies.append(pltpu.make_async_copy(momenta_in, momenta_ref, sems.at[1]))
    for copy in copies:
        copy.start()
    for q in range(6):
        copies[q].wait()
        rows = pl.ds(q * side, side)
        low_x[rows, :] = v_ref[q // 3, q % 3, :side, :]
        for h in range(v32.shape[0]):
            at = slice(h * LANES, (h + 1) * LANES)
            v32[h] = v_ref[q // 3, q % 3, :, at].astype(F32)
            low_y[rows, at] = v32[h, pl.ds(0, side, stride=side), :].astype(BF16)
            high_y[rows, at] = v32[h, pl.ds(side - 1, side, stride=side), :].astype(BF16)
    copies[6].wait()
    copies[7].wait()


def turn(product, extent):
    return product - extent * jnp.floor(product / extent)


def phase_rows(momenta_ref, gx, gy, gz):
    np_ = momenta_ref.shape[1]
    row = lax.broadcasted_iota(jnp.int32, (np_, np_), 0)
    lane = lax.broadcasted_iota(jnp.int32, (np_, np_), 1)

    def column(n):
        values = jnp.broadcast_to(momenta_ref[n : n + 1, :].astype(F32), (np_, np_))
        return jnp.sum(jnp.where(row == lane, values, 0.0), 1, keepdims=True)

    total = turn(column(0) * gx, NX) / NX + turn(column(1) * gy, NY) / NY + turn(column(2) * gz, ZEXT) / ZEXT
    angle = 2.0 * math.pi * total
    return jnp.cos(angle), jnp.sin(angle)


def dot_t(a, b):
    return lax.dot_general(a, b, (((1,), (1,)), ((), ())), preferred_element_type=F32)


def identity(size):
    row = lax.broadcasted_iota(jnp.int32, (size, size), 0)
    lane = lax.broadcasted_iota(jnp.int32, (size, size), 1)
    return jnp.where(row == lane, 1.0, 0.0).astype(BF16)


def put(coef, app, i, j, re, im):
    for n, value in enumerate((re, im, re + im)):
        coef[app * 27 + n * 9 + 3 * i + j] = jnp.broadcast_to(value, coef.shape[1:])


def place_of(q, t, tiles):
    if t < tiles - 1:
        return q * (tiles - 1) + t
    return 3 * (tiles - 1) + q


def displace_tile(apps, skip_diagonal=False):
    def pair(links, app, n, i, j, cols):
        c = links[app * 27 + n * 9 + 3 * i + j, :, cols]
        return jnp.concatenate([c, c], 0)

    def add(a, b):
        return b if a is None else a + b

    joined = [[vec[j] + vec[3 + j] for j in range(3)] for _, _, _, vec in apps]
    out = [None] * 6
    for i in range(3):
        p1 = p2 = p3 = None
        for (links, app, cols, vec), both in zip(apps, joined):
            for j in range(3):
                if not (skip_diagonal and i == j):
                    p1 = add(p1, pair(links, app, 0, i, j, cols) * vec[j])
                p2 = add(p2, pair(links, app, 1, i, j, cols) * vec[3 + j])
                p3 = add(p3, pair(links, app, 2, i, j, cols) * both[j])
        out[i] = p1 - p2
        out[3 + i] = p3 - p1 - p2
    return out


def store_tile(ref, d, n, q_places, count, values):
    for q in range(6):
        rows = pl.ds(pl.multiple_of((q // 3) * count + n * 16, 16), 16)
        at = slice(q_places[q % 3] * LANES, (q_places[q % 3] + 1) * LANES)
        ref[d, rows, at] = values[q].astype(BF16)


def interior_kernel(side, z_blocks, momenta_ref, v_ref, u_ref, *rest):
    if z_blocks > 1:
        z_up_ref, z_down_ref, u_down_ref = rest[:3]
        rest = rest[3:]
        vz = rest[5]
        rest = rest[:5] + rest[6:]
    vp, tab, last_tab, coef, side_coef, inner_ref, vs = rest
    me = lax.axis_index("gz")
    block_z = (me // 16).astype(F32)
    x0 = (me // 4 % 4 * side).astype(F32)
    y0 = (me % 4 * side).astype(F32)
    sites = v_ref.shape[2]
    count = v_ref.shape[3]
    wide = vp.shape[-1]
    tiles = wide // LANES
    tail = sites - wide + LANES
    np_ = momenta_ref.shape[1]

    lane = lax.broadcasted_iota(jnp.int32, (np_, wide), 1)
    xl = (lane // side).astype(F32)
    yl = (lane % side).astype(F32)
    c_rows, s_rows = phase_rows(momenta_ref, x0 + xl, y0 + yl, block_z)
    tab[0] = c_rows
    tab[1] = s_rows
    final = slice(wide - LANES, wide)
    behind = lane[:, final] - sites
    k = (behind % side).astype(F32)
    for d in range(3):
        if d == 0:
            gx, gy = x0 + float(side), y0 + k
        else:
            gx, gy = x0 + k, y0 + jnp.where(behind < side, float(side - 1), float(side))
        c_face, s_face = phase_rows(momenta_ref, gx, gy, block_z)
        last_tab[d, 0] = jnp.where(behind < 0, c_rows[:, final], c_face)
        last_tab[d, 1] = jnp.where(behind < 0, s_rows[:, final], s_face)

    unit = identity(count)
    for q in range(6):
        vp[q, :, wide - LANES :] = jnp.zeros((count, LANES), F32)
        vp[q, :, :sites] = dot_t(unit, v_ref[q // 3, q % 3])

    lane1 = lax.broadcasted_iota(jnp.int32, (1, wide), 1)
    inside = lane1 < sites
    masks = (
        (inside, lane1 < sites + side),
        (inside & (lane1 % side != side - 1), inside & (lane1 % side != 0)),
    )
    for d in range(2):
        rows = wide_row(link_rows(u_ref, d) * 0.5, wide)
        ahead = jnp.where(masks[d][0], rows, 0.0)
        back = jnp.where(masks[d][1], pltpu.roll(rows, (side, 1)[d], 1), 0.0)
        for i in range(3):
            for j in range(3):
                n = (3 * i + j) * 2
                put(coef, 2 * d, i, j, ahead[n : n + 1], ahead[n + 1 : n + 2])
                put(coef, 2 * d + 1, j, i, -back[n : n + 1], back[n + 1 : n + 2])
    site = lax.broadcasted_iota(jnp.int32, (sites, LANES), 0)
    place = lax.broadcasted_iota(jnp.int32, (sites, LANES), 1) - tail
    hit = (site == place % side * side + side - 1) & (place >= 0) & (place < 2 * side)
    pick = jnp.where(hit, 1.0, 0.0).astype(BF16)
    near = 0.5 * jnp.dot(link_rows(u_ref, 1).astype(BF16), pick, preferred_element_type=F32)
    forward = lane1[:, :LANES] < tail + side
    for i in range(3):
        for j in range(3):
            n = (3 * i + j) * 2
            m = (3 * j + i) * 2
            re = jnp.where(forward, near[n : n + 1], -near[m : m + 1])
            put(side_coef, 0, i, j, re, jnp.where(forward, near[n + 1 : n + 2], near[m + 1 : m + 2]))
    rows = wide_row(link_rows(u_ref, 2) * 0.5, wide)
    if z_blocks > 1:
        back = wide_row(link_rows(u_down_ref, 0) * 0.5, wide)
    for i in range(3):
        for j in range(3):
            n = (3 * i + j) * 2
            m = (3 * j + i) * 2
            if z_blocks > 1:
                put(coef, 4, i, j, rows[n : n + 1], rows[n + 1 : n + 2])
                put(coef, 5, j, i, -back[n : n + 1], back[n + 1 : n + 2])
            else:
                put(coef, 4, i, j, rows[n : n + 1] - rows[m : m + 1], rows[n + 1 : n + 2] + rows[m + 1 : m + 2])
    if z_blocks > 1:
        for q in range(6):
            for m, ref in enumerate((z_up_ref, z_down_ref)):
                vz[m, q, :, wide - LANES :] = jnp.zeros((count, LANES), BF16)
                vz[m, q, :, :sites] = dot_t(unit, ref[q // 3, q % 3]).astype(BF16)

    shifts = (wide - side, side, wide - 1, 1)

    def displace(n, carry):
        rows = pl.ds(pl.multiple_of(n * 16, 16), 16)
        for q in range(6):
            value = vp[q, rows, :]
            for m, amount in enumerate(shifts):
                vs[m, q] = pltpu.roll(value, amount, 1)
        for t in range(tiles - 1):
            cols = slice(t * LANES, (t + 1) * LANES)
            spots = [place_of(q, t, tiles) for q in range(3)]
            for d in range(2):
                apps = [(coef, 2 * d + m, cols, [vs[2 * d + m, q, :, cols] for q in range(6)]) for m in range(2)]
                store_tile(inner_ref, d, n, spots, count, displace_tile(apps))
            if z_blocks == 1:
                vec = [vp[q, rows, cols] for q in range(6)]
                values = displace_tile([(coef, 4, cols, vec)], True)
            else:
                apps = [(coef, 4 + m, cols, [vz[m, q, rows, cols].astype(F32) for q in range(6)]) for m in range(2)]
                values = displace_tile(apps)
            store_tile(inner_ref, 2, n, spots, count, values)
        return carry

    lax.fori_loop(0, count // 16, displace, 0)


def border(side, sites, vp, vz, coef, side_coef, high_y, halo_x, halo_y, outer, last, halo_t):
    count = vp.shape[1]
    wide = vp.shape[-1]
    tail = sites - wide + LANES
    final = slice(wide - LANES, wide)
    unit = identity(count)
    for q in range(6):
        at = slice(q * side, (q + 1) * side)
        pieces = [jnp.zeros((tail - side, count), F32)]
        pieces += [ref[at, :].astype(F32) for ref in (halo_x, halo_y, high_y)]
        pieces.append(jnp.zeros((LANES - tail - 2 * side, count), F32))
        halo_t[q] = dot_t(unit, jnp.concatenate(pieces, 0).astype(BF16))
    lane16 = lax.broadcasted_iota(jnp.int32, (16, LANES), 1)
    alone = slice(0, LANES)
    inside = lane16 < tail

    def one(n, carry):
        rows = pl.ds(pl.multiple_of(n * 16, 16), 16)
        end = [vp[q, rows, wide - 2 * LANES : wide] for q in range(6)]
        spots = [0, 1, 2]
        got = [halo_t[q, rows, :] for q in range(6)]
        ahead = [jnp.where(lane16 >= tail - side, g, pltpu.roll(a[:, LANES:], LANES - side, 1)) for a, g in zip(end, got)]
        behind = [pltpu.roll(a, side, 1)[:, LANES:] for a in end]
        store_tile(outer, 0, n, spots, count, displace_tile([(coef, 0, final, ahead), (coef, 1, final, behind)]))
        ahead = [pltpu.roll(a[:, LANES:], LANES - 1, 1) for a in end]
        behind = [pltpu.roll(a, 1, 1)[:, LANES:] for a in end]
        apps = [(coef, 2, final, ahead), (coef, 3, final, behind), (side_coef, 0, alone, got)]
        store_tile(outer, 1, n, spots, count, displace_tile(apps))
        if vz is None:
            values = displace_tile([(coef, 4, final, [a[:, LANES:] for a in end])], True)
        else:
            values = displace_tile([(coef, 4 + m, final, [vz[m, q, rows, final].astype(F32) for q in range(6)]) for m in range(2)])
        store_tile(outer, 2, n, spots, count, values)
        for q in range(6):
            own = end[q][:, LANES:]
            up = pltpu.roll(got[q], side, 1)
            down = pltpu.roll(got[q], LANES - side, 1)
            last[0, q, rows, :] = jnp.where(inside, own, up)
            last[1, q, rows, :] = jnp.where(inside, own, jnp.where(lane16 < tail + side, down, up))
            last[2, q, rows, :] = own
        return carry

    lax.fori_loop(0, count // 16, one, 0)


def products_kernel(
    side, sites, z_blocks, factor, start, stop, with_border, directions_ref, vp, tab, last_tab, inner_ref, *rest
):
    me = lax.axis_index("gz")
    if with_border:
        coef, side_coef, high_y, halo_x, halo_y = rest[:5]
        rest = rest[5:]
        vz = None
        if z_blocks > 1:
            vz = rest[0]
            rest = rest[1:]
        keep_ref, send_ref, outer, last, left_a, left_b, acc, halo_t = rest
        border(side, sites, vp, vz, coef, side_coef, high_y, halo_x, halo_y, outer, last, halo_t)
    else:
        outer, last = rest[:2]
        rest = rest[2:]
        done = ()
        if len(rest) == 7:
            done = rest[:2]
            rest = rest[2:]
        keep_ref, send_ref, left_a, left_b, acc = rest
    count = vp.shape[1]
    tiles = vp.shape[2] // LANES
    cut = 3 * (tiles - 1) * LANES
    mine = me % 2

    def make_left(p, ref, n):
        rows = pl.ds(n * 16, 16)
        lower = pl.ds(count + n * 16, 16)
        for t in range(tiles):
            cols = slice(t * LANES, (t + 1) * LANES)
            end = t == tiles - 1
            d = directions_ref[p]
            c, s = ((last_tab[d, m, p : p + 1, :] if end else tab[m, p : p + 1, cols]) for m in range(2))
            c = jnp.broadcast_to(c, (16, LANES))
            s = jnp.broadcast_to(s, (16, LANES))
            for q in range(3):
                vr, vi = (last[d, 3 * r + q, rows, :] if end else vp[3 * r + q, rows, cols] for r in range(2))
                spot = place_of(q, t, tiles)
                at = slice(spot * LANES, (spot + 1) * LANES)
                ref[rows, at] = (vr * c + vi * s).astype(BF16)
                ref[lower, at] = (vr * s - vi * c).astype(BF16)

    base = start
    if not with_border and done:
        before = done[0].shape[0]
        keep_ref[:before] = done[0][...]
        send_ref[:before] = done[1][...]
        base = start - before
    steps = count // 16
    lefts = (left_a, left_b)
    for n in range(steps):
        make_left(start, left_a, n)
    for p in range(start, stop):
        d = directions_ref[p]
        left = lefts[(p - start) % 2]
        later = lefts[(p + 1 - start) % 2]
        x = dot_t(left[:count, :cut], inner_ref[d]) + dot_t(left[:count, cut:], outer[d])
        if p + 1 < stop:
            for n in range(steps // 2):
                make_left(p + 1, later, n)
        y = dot_t(left[count:, :cut], inner_ref[d]) + dot_t(left[count:, cut:], outer[d])
        if p + 1 < stop:
            for n in range(steps // 2, steps):
                make_left(p + 1, later, n)
        acc[0] = ((x[:, :count] - y[:, count:]) * factor).reshape(acc.shape[1:])
        acc[1] = ((x[:, count:] + y[:, :count]) * factor).reshape(acc.shape[1:])
        for form in range(2):
            keep_ref[p - base, form] = acc[form, :, mine]
            send_ref[p - base, form] = acc[form, :, 1 - mine].astype(BF16)


def halve_kernel(following, keep_ref, got_ref, *outs):
    mine = lax.axis_index("gz") // following % 2
    inner_ref, send_ref = outs
    inner_ref[...] = keep_ref[:, :, mine] + got_ref[:, :, mine].astype(F32)
    send_ref[...] = (keep_ref[:, :, 1 - mine] + got_ref[:, :, 1 - mine].astype(F32)).astype(BF16)


def exchange(send, bit):
    return lax.ppermute(send, "gz", [(i, i ^ bit) for i in range(lax.axis_size("gz"))])


def halve(keep, got, following, bits):
    vmem = pl.BlockSpec(memory_space=pltpu.VMEM)
    lead = keep.shape[0] * 2
    rows, columns = keep.shape[2:]
    outer = 2 ** bits.index(following)
    bits.remove(following)
    split = (lead, outer, 2, rows // (2 * outer), columns)
    half = (lead, outer, rows // (2 * outer), columns)
    keep, send = pl.pallas_call(
        functools.partial(halve_kernel, following),
        out_shape=[jax.ShapeDtypeStruct(half, F32), jax.ShapeDtypeStruct(half, BF16)],
        in_specs=[vmem] * 2,
        out_specs=[vmem] * 2,
        compiler_params=pltpu.CompilerParams(vmem_limit_bytes=VMEM_LIMIT),
    )(keep.reshape(split), got.reshape(split))
    shape = (lead // 2, 2, rows // 2, columns)
    return keep.reshape(shape), send.reshape(shape)


def finish_kernel(*refs):
    out_ref = refs[-1]
    at = 0
    for keep_ref, got_ref in zip(refs[0:-1:2], refs[1:-1:2]):
        size = keep_ref.shape[0]
        out_ref[at : at + size] = keep_ref[...] + got_ref[...].astype(F32)
        at += size


def body(eigvecs, gauge_links, momenta, directions):
    device_count = lax.axis_size("gz")
    v = jnp.swapaxes(eigvecs[0], 2, 3)
    u = jnp.transpose(gauge_links[0], (0, 2, 3, 1, 4))
    side = NX // 4
    sites, count = v.shape[2:]
    z_blocks = device_count // 16
    wide = -(-sites // LANES) * LANES
    tiles = wide // LANES
    tail = sites - wide + LANES
    if sites != side * (NY // 4) or device_count & (device_count - 1) or count % device_count:
        raise ValueError("unsupported block")
    if tiles < 3 or tail < 2 * side or tail + 2 * side > LANES:
        raise ValueError("unsupported sites")
    np_ = momenta.shape[0]
    factor = (3.0 * NX * NY * z_blocks) ** (-0.5)
    vmem = pl.BlockSpec(memory_space=pltpu.VMEM)
    smem = pl.BlockSpec(memory_space=pltpu.SMEM)
    params = pltpu.CompilerParams(vmem_limit_bytes=VMEM_LIMIT)
    face = jax.ShapeDtypeStruct((6 * side, count), BF16)
    arguments = [pltpu.with_memory_space_constraint(x, pltpu.HBM) for x in (momenta.T, v, u)]
    near_momenta, near_v, near_u, low_x, low_y, high_y = pl.pallas_call(
        functools.partial(faces_kernel, side),
        out_shape=[jax.ShapeDtypeStruct(x.shape, x.dtype) for x in arguments] + [face] * 3,
        in_specs=[pl.BlockSpec(memory_space=pltpu.HBM)] * 3,
        out_specs=[vmem] * 6,
        scratch_shapes=[
            pltpu.VMEM((count // LANES, sites, LANES), F32),
            pltpu.SemaphoreType.DMA((6,)),
            pltpu.SemaphoreType.DMA((2,)),
        ],
        compiler_params=pltpu.CompilerParams(vmem_limit_bytes=FACES_LIMIT),
        name="faces",
    )(*arguments)

    def sent(face, stride, sign):
        of = side_route(stride, sign)
        return lax.ppermute(face, "gz", [(i, of(i)) for i in range(device_count)])

    halos = [sent(low_x, 4, -1), sent(low_y, 1, -1)]
    applications = 6 if z_blocks > 1 else 5
    operands = [near_momenta, near_v, near_u]
    shapes = [
        jax.ShapeDtypeStruct((6, count, wide), F32),
        jax.ShapeDtypeStruct((2, np_, wide), F32),
        jax.ShapeDtypeStruct((3, 2, np_, LANES), F32),
        jax.ShapeDtypeStruct((applications * 27, 8, wide), F32),
        jax.ShapeDtypeStruct((27, 8, LANES), F32),
    ]
    if z_blocks > 1:
        operands += [
            lax.ppermute(v, "gz", route(device_count, -16)),
            lax.ppermute(v, "gz", route(device_count, 16)),
            lax.ppermute(u[2:3], "gz", route(device_count, 16)),
        ]
        shapes.append(jax.ShapeDtypeStruct((2, 6, count, wide), BF16))
    shapes.append(jax.ShapeDtypeStruct((3, 2 * count, 3 * (tiles - 1) * LANES), BF16))
    results = pl.pallas_call(
        functools.partial(interior_kernel, side, z_blocks),
        out_shape=shapes,
        in_specs=[vmem] * len(operands),
        out_specs=[vmem] * len(shapes),
        scratch_shapes=[pltpu.VMEM((4, 6, 16, wide), F32)],
        compiler_params=params,
        name="interior",
    )(*operands)
    vp, tab, last_tab, coef, side_coef = results[:5]
    inner = results[-1]
    vz = list(results[5:-1])
    half = count // 2
    per = count // device_count
    lead = (device_count // 2, per, count)

    def products(start, stop, extra, table, done=()):
        with_border = not start
        extra = [*extra, *done]
        size = stop - start + (done[0].shape[0] if done else 0)
        operands = [directions, vp, table, last_tab, inner, *extra]
        shapes = [
            jax.ShapeDtypeStruct((size, 2) + lead, F32),
            jax.ShapeDtypeStruct((size, 2) + lead, BF16),
        ]
        scratch = [
            pltpu.VMEM((2 * count, 3 * wide), BF16),
            pltpu.VMEM((2 * count, 3 * wide), BF16),
            pltpu.VMEM((2, device_count // 2, 2, per, count), F32),
        ]
        if with_border:
            shapes.append(jax.ShapeDtypeStruct((3, 2 * count, 3 * LANES), BF16))
            shapes.append(jax.ShapeDtypeStruct((3, 6, count, LANES), F32))
            scratch.append(pltpu.VMEM((6, count, LANES), F32))
        results = pl.pallas_call(
            functools.partial(products_kernel, side, sites, z_blocks, factor, start, stop, with_border),
            out_shape=shapes,
            in_specs=[smem] + [vmem] * (len(operands) - 1),
            out_specs=[vmem] * len(shapes),
            scratch_shapes=scratch,
            compiler_params=params,
        )(*operands)
        return results[0], results[1], results[2:]

    def flat(x):
        return x.reshape(x.shape[:2] + (half, count))

    order = [2**n for n in range(device_count.bit_length() - 1)]
    other = order
    cut, between = np_ * CUTS[0] // 8, np_ * CUTS[1] // 8
    bits_a, bits_b = order[:0:-1], order[:0:-1]
    keep_a, send_a, behind = products(0, cut, [coef, side_coef, high_y, *halos, *vz], tab)
    keep_a = flat(keep_a)
    got_a = exchange(flat(send_a), order[0])
    done = products(cut, between, behind, tab)[:2]
    got_a, send_b = lax.optimization_barrier((got_a, done[1]))
    keep_a, send_a = halve(keep_a, got_a, order[1], bits_a)
    send_a, table = lax.optimization_barrier((send_a, tab))
    got_a = exchange(send_a, order[1])
    keep_b, send_b, _ = products(between, np_, behind, table, (done[0], send_b))
    keep_b = flat(keep_b)
    got_b = exchange(flat(send_b), other[0])
    for n in range(1, len(order)):
        keep_b, send_b = halve(keep_b, got_b, other[n], bits_b)
        got_b = exchange(send_b, other[n])
        if n + 1 < len(order):
            keep_a, send_a = halve(keep_a, got_a, order[n + 1], bits_a)
            got_a = exchange(send_a, order[n + 1])
    return pl.pallas_call(
        finish_kernel,
        out_shape=jax.ShapeDtypeStruct((np_,) + keep_a.shape[1:], F32),
        in_specs=[vmem] * 4,
        out_specs=vmem,
        compiler_params=params,
        name="finish",
    )(keep_a, got_a, keep_b, got_b)


def solution(mesh):
    return jax.shard_map(
        body,
        mesh=mesh,
        in_specs=(
            P(("slab", "gz"), None, None, None, None),
            P(("slab", "gz"), None, None, None, None, None),
            P(),
            P(),
        ),
        out_specs=P("slab", None, "gz", None),
        check_vma=False,
    )
```

```python
import functools
import math

import jax
import jax.numpy as jnp
from jax import lax
from jax.experimental import pallas as pl
from jax.experimental.pallas import tpu as pltpu
from jax.sharding import PartitionSpec as P

NX = 96
NY = 96
ZEXT = 96

LANES = 128
VMEM_LIMIT = 30 * 2**20
CUTS = (5, 7)
FACES_LIMIT = 30 * 2**20
F32 = jnp.float32
BF16 = jnp.bfloat16


def route(count, shift):
    return [(i, (i + shift) % count) for i in range(count)]


def side_route(stride, sign):
    def of(i):
        here = i // stride % 4
        return i + ((here + sign) % 4 - here) * stride

    return of


def wide_row(rows, wide):
    pad = jnp.zeros((rows.shape[0], wide - rows.shape[1]), F32)
    return jnp.concatenate([rows, pad], 1)


def link_rows(ref, d):
    return jnp.concatenate([ref[d, i, j].astype(F32) for i in range(3) for j in range(3)], 0)


def faces_kernel(
    side, momenta_in, v_in, u_in, momenta_ref, v_ref, u_ref, low_x, low_y, high_y, v32, v_sems, sems
):
    copies = [
        pltpu.make_async_copy(v_in.at[q // 3, q % 3], v_ref.at[q // 3, q % 3], v_sems.at[q]) for q in range(6)
    ]
    copies.append(pltpu.make_async_copy(u_in, u_ref, sems.at[0]))
    copies.append(pltpu.make_async_copy(momenta_in, momenta_ref, sems.at[1]))
    for copy in copies:
        copy.start()
    for q in range(6):
        copies[q].wait()
        rows = pl.ds(q * side, side)
        low_x[rows, :] = v_ref[q // 3, q % 3, :side, :]
        for h in range(v32.shape[0]):
            at = slice(h * LANES, (h + 1) * LANES)
            v32[h] = v_ref[q // 3, q % 3, :, at].astype(F32)
            low_y[rows, at] = v32[h, pl.ds(0, side, stride=side), :].astype(BF16)
            high_y[rows, at] = v32[h, pl.ds(side - 1, side, stride=side), :].astype(BF16)
    copies[6].wait()
    copies[7].wait()


def turn(product, extent):
    return product - extent * jnp.floor(product / extent)


def phase_rows(momenta_ref, gx, gy, gz):
    np_ = momenta_ref.shape[1]
    row = lax.broadcasted_iota(jnp.int32, (np_, np_), 0)
    lane = lax.broadcasted_iota(jnp.int32, (np_, np_), 1)

    def column(n):
        values = jnp.broadcast_to(momenta_ref[n : n + 1, :].astype(F32), (np_, np_))
        return jnp.sum(jnp.where(row == lane, values, 0.0), 1, keepdims=True)

    total = turn(column(0) * gx, NX) / NX + turn(column(1) * gy, NY) / NY + turn(column(2) * gz, ZEXT) / ZEXT
    angle = 2.0 * math.pi * total
    return jnp.cos(angle), jnp.sin(angle)


def dot_t(a, b):
    return lax.dot_general(a, b, (((1,), (1,)), ((), ())), preferred_element_type=F32)


def identity(size):
    row = lax.broadcasted_iota(jnp.int32, (size, size), 0)
    lane = lax.broadcasted_iota(jnp.int32, (size, size), 1)
    return jnp.where(row == lane, 1.0, 0.0).astype(BF16)


def sixteen(n):
    return pl.ds(n * 16, 16) if isinstance(n, int) else pl.ds(pl.multiple_of(n * 16, 16), 16)


def put(coef, app, i, j, re, im):
    for n, value in enumerate((re, im, re + im)):
        coef[app * 27 + n * 9 + 3 * i + j] = jnp.broadcast_to(value, coef.shape[1:])


def place_of(q, t, tiles):
    if t < tiles - 1:
        return q * (tiles - 1) + t
    return 3 * (tiles - 1) + q


def displace_tile(apps, skip_diagonal=False):
    def pair(links, app, n, i, j, cols):
        c = links[app * 27 + n * 9 + 3 * i + j, :, cols]
        return jnp.concatenate([c, c], 0)

    def add(a, b):
        return b if a is None else a + b

    joined = [[vec[j] + vec[3 + j] for j in range(3)] for _, _, _, vec in apps]
    out = [None] * 6
    for i in range(3):
        p1 = p2 = p3 = None
        for (links, app, cols, vec), both in zip(apps, joined):
            for j in range(3):
                if not (skip_diagonal and i == j):
                    p1 = add(p1, pair(links, app, 0, i, j, cols) * vec[j])
                p2 = add(p2, pair(links, app, 1, i, j, cols) * vec[3 + j])
                p3 = add(p3, pair(links, app, 2, i, j, cols) * both[j])
        out[i] = p1 - p2
        out[3 + i] = p3 - p1 - p2
    return out


def store_tile(ref, d, n, q_places, count, values):
    for q in range(6):
        rows = sixteen((q // 3) * (count // 16) + n)
        at = slice(q_places[q % 3] * LANES, (q_places[q % 3] + 1) * LANES)
        ref[d, rows, at] = values[q].astype(BF16)


def interior_kernel(side, z_blocks, momenta_ref, v_ref, u_ref, *rest):
    if z_blocks > 1:
        z_up_ref, z_down_ref, u_down_ref = rest[:3]
        rest = rest[3:]
        vz = rest[5]
        rest = rest[:5] + rest[6:]
    vp, tab, last_tab, coef, side_coef, inner_ref, vs = rest
    me = lax.axis_index("gz")
    block_z = (me // 16).astype(F32)
    x0 = (me // 4 % 4 * side).astype(F32)
    y0 = (me % 4 * side).astype(F32)
    sites = v_ref.shape[2]
    count = v_ref.shape[3]
    wide = vp.shape[-1]
    tiles = wide // LANES
    tail = sites - wide + LANES
    np_ = momenta_ref.shape[1]

    lane = lax.broadcasted_iota(jnp.int32, (np_, wide), 1)
    xl = (lane // side).astype(F32)
    yl = (lane % side).astype(F32)
    c_rows, s_rows = phase_rows(momenta_ref, x0 + xl, y0 + yl, block_z)
    tab[0] = c_rows
    tab[1] = s_rows
    final = slice(wide - LANES, wide)
    behind = lane[:, final] - sites
    k = (behind % side).astype(F32)
    for d in range(3):
        if d == 0:
            gx, gy = x0 + float(side), y0 + k
        else:
            gx, gy = x0 + k, y0 + jnp.where(behind < side, float(side - 1), float(side))
        c_face, s_face = phase_rows(momenta_ref, gx, gy, block_z)
        last_tab[d, 0] = jnp.where(behind < 0, c_rows[:, final], c_face)
        last_tab[d, 1] = jnp.where(behind < 0, s_rows[:, final], s_face)

    unit = identity(count)
    for q in range(6):
        vp[q, :, wide - LANES :] = jnp.zeros((count, LANES), F32)
        vp[q, :, :sites] = dot_t(unit, v_ref[q // 3, q % 3])

    lane1 = lax.broadcasted_iota(jnp.int32, (1, wide), 1)
    inside = lane1 < sites
    masks = (
        (inside, lane1 < sites + side),
        (inside & (lane1 % side != side - 1), inside & (lane1 % side != 0)),
    )
    for d in range(2):
        rows = wide_row(link_rows(u_ref, d) * 0.5, wide)
        ahead = jnp.where(masks[d][0], rows, 0.0)
        back = jnp.where(masks[d][1], pltpu.roll(rows, (side, 1)[d], 1), 0.0)
        for i in range(3):
            for j in range(3):
                n = (3 * i + j) * 2
                put(coef, 2 * d, i, j, ahead[n : n + 1], ahead[n + 1 : n + 2])
                put(coef, 2 * d + 1, j, i, -back[n : n + 1], back[n + 1 : n + 2])
    site = lax.broadcasted_iota(jnp.int32, (sites, LANES), 0)
    place = lax.broadcasted_iota(jnp.int32, (sites, LANES), 1) - tail
    hit = (site == place % side * side + side - 1) & (place >= 0) & (place < 2 * side)
    pick = jnp.where(hit, 1.0, 0.0).astype(BF16)
    near = 0.5 * jnp.dot(link_rows(u_ref, 1).astype(BF16), pick, preferred_element_type=F32)
    forward = lane1[:, :LANES] < tail + side
    for i in range(3):
        for j in range(3):
            n = (3 * i + j) * 2
            m = (3 * j + i) * 2
            re = jnp.where(forward, near[n : n + 1], -near[m : m + 1])
            put(side_coef, 0, i, j, re, jnp.where(forward, near[n + 1 : n + 2], near[m + 1 : m + 2]))
    rows = wide_row(link_rows(u_ref, 2) * 0.5, wide)
    if z_blocks > 1:
        back = wide_row(link_rows(u_down_ref, 0) * 0.5, wide)
    for i in range(3):
        for j in range(3):
            n = (3 * i + j) * 2
            m = (3 * j + i) * 2
            if z_blocks > 1:
                put(coef, 4, i, j, rows[n : n + 1], rows[n + 1 : n + 2])
                put(coef, 5, j, i, -back[n : n + 1], back[n + 1 : n + 2])
            else:
                put(coef, 4, i, j, rows[n : n + 1] - rows[m : m + 1], rows[n + 1 : n + 2] + rows[m + 1 : m + 2])
    if z_blocks > 1:
        for q in range(6):
            for m, ref in enumerate((z_up_ref, z_down_ref)):
                vz[m, q, :, wide - LANES :] = jnp.zeros((count, LANES), BF16)
                vz[m, q, :, :sites] = dot_t(unit, ref[q // 3, q % 3]).astype(BF16)

    shifts = (wide - side, side, wide - 1, 1)

    def displace(n, carry):
        rows = pl.ds(pl.multiple_of(n * 16, 16), 16)
        for q in range(6):
            value = vp[q, rows, :]
            for m, amount in enumerate(shifts):
                vs[m, q] = pltpu.roll(value, amount, 1)
        for t in range(tiles - 1):
            cols = slice(t * LANES, (t + 1) * LANES)
            spots = [place_of(q, t, tiles) for q in range(3)]
            for d in range(2):
                apps = [(coef, 2 * d + m, cols, [vs[2 * d + m, q, :, cols] for q in range(6)]) for m in range(2)]
                store_tile(inner_ref, d, n, spots, count, displace_tile(apps))
            if z_blocks == 1:
                vec = [vp[q, rows, cols] for q in range(6)]
                values = displace_tile([(coef, 4, cols, vec)], True)
            else:
                apps = [(coef, 4 + m, cols, [vz[m, q, rows, cols].astype(F32) for q in range(6)]) for m in range(2)]
                values = displace_tile(apps)
            store_tile(inner_ref, 2, n, spots, count, values)
        return carry

    lax.fori_loop(0, count // 16, displace, 0)


def border(side, sites, vp, vz, coef, side_coef, high_y, halo_x, halo_y, outer, last, halo_t):
    count = vp.shape[1]
    wide = vp.shape[-1]
    tail = sites - wide + LANES
    final = slice(wide - LANES, wide)
    unit = identity(count)
    for q in range(6):
        at = slice(q * side, (q + 1) * side)
        pieces = [jnp.zeros((tail - side, count), F32)]
        pieces += [ref[at, :].astype(F32) for ref in (halo_x, halo_y, high_y)]
        pieces.append(jnp.zeros((LANES - tail - 2 * side, count), F32))
        halo_t[q] = dot_t(unit, jnp.concatenate(pieces, 0).astype(BF16))
    lane16 = lax.broadcasted_iota(jnp.int32, (16, LANES), 1)
    alone = slice(0, LANES)
    inside = lane16 < tail

    def one(n):
        rows = sixteen(n)
        end = [vp[q, rows, wide - 2 * LANES : wide] for q in range(6)]
        spots = [0, 1, 2]
        got = [halo_t[q, rows, :] for q in range(6)]
        ahead = [jnp.where(lane16 >= tail - side, g, pltpu.roll(a[:, LANES:], LANES - side, 1)) for a, g in zip(end, got)]
        behind = [pltpu.roll(a, side, 1)[:, LANES:] for a in end]
        store_tile(outer, 0, n, spots, count, displace_tile([(coef, 0, final, ahead), (coef, 1, final, behind)]))
        ahead = [pltpu.roll(a[:, LANES:], LANES - 1, 1) for a in end]
        behind = [pltpu.roll(a, 1, 1)[:, LANES:] for a in end]
        apps = [(coef, 2, final, ahead), (coef, 3, final, behind), (side_coef, 0, alone, got)]
        store_tile(outer, 1, n, spots, count, displace_tile(apps))
        if vz is None:
            values = displace_tile([(coef, 4, final, [a[:, LANES:] for a in end])], True)
        else:
            values = displace_tile([(coef, 4 + m, final, [vz[m, q, rows, final].astype(F32) for q in range(6)]) for m in range(2)])
        store_tile(outer, 2, n, spots, count, values)
        for q in range(6):
            own = end[q][:, LANES:]
            up = pltpu.roll(got[q], side, 1)
            down = pltpu.roll(got[q], LANES - side, 1)
            last[0, q, rows, :] = jnp.where(inside, own, up)
            last[1, q, rows, :] = jnp.where(inside, own, jnp.where(lane16 < tail + side, down, up))
            last[2, q, rows, :] = own

    return one


def products_kernel(
    side, sites, z_blocks, factor, start, stop, with_border, directions_ref, vp, tab, last_tab, inner_ref, *rest
):
    me = lax.axis_index("gz")
    if with_border:
        coef, side_coef, high_y, halo_x, halo_y = rest[:5]
        rest = rest[5:]
        vz = None
        if z_blocks > 1:
            vz = rest[0]
            rest = rest[1:]
        keep_ref, send_ref, outer, last, left_a, left_b, acc, halo_t, sums = rest
        displace = border(side, sites, vp, vz, coef, side_coef, high_y, halo_x, halo_y, outer, last, halo_t)
    else:
        outer, last = rest[:2]
        rest = rest[2:]
        done = ()
        if len(rest) == 7:
            done = rest[:2]
            rest = rest[2:]
        keep_ref, send_ref, left_a, left_b, acc = rest
    count = vp.shape[1]
    tiles = vp.shape[2] // LANES
    cut = 3 * (tiles - 1) * LANES
    mine = me % 2

    def make_left(p, ref, n, some):
        rows = pl.ds(n * 16, 16)
        lower = pl.ds(count + n * 16, 16)
        for t in some:
            cols = slice(t * LANES, (t + 1) * LANES)
            end = t == tiles - 1
            d = directions_ref[p]
            c, s = ((last_tab[d, m, p : p + 1, :] if end else tab[m, p : p + 1, cols]) for m in range(2))
            c = jnp.broadcast_to(c, (16, LANES))
            s = jnp.broadcast_to(s, (16, LANES))
            for q in range(3):
                vr, vi = (last[d, 3 * r + q, rows, :] if end else vp[3 * r + q, rows, cols] for r in range(2))
                spot = place_of(q, t, tiles)
                at = slice(spot * LANES, (spot + 1) * LANES)
                ref[rows, at] = (vr * c + vi * s).astype(BF16)
                ref[lower, at] = (vr * s - vi * c).astype(BF16)

    base = start
    if not with_border and done:
        before = done[0].shape[0]
        keep_ref[:before] = done[0][...]
        send_ref[:before] = done[1][...]
        base = start - before
    steps = count // 16
    lefts = (left_a, left_b)
    inner_tiles, last_tiles, all_tiles = range(tiles - 1), [tiles - 1], range(tiles)
    inner_columns, last_columns = slice(0, cut), slice(cut, 3 * tiles * LANES)

    def product(rows, ref, columns, right):
        return dot_t(ref[rows, columns], right)

    upper, lower_rows = slice(0, count), slice(count, 2 * count)

    def write(p, real, imag):
        acc[0] = (real * factor).reshape(acc.shape[1:])
        acc[1] = (imag * factor).reshape(acc.shape[1:])
        for form in range(2):
            keep_ref[p - base, form] = acc[form, :, mine]
            send_ref[p - base, form] = acc[form, :, 1 - mine].astype(BF16)

    early = 0
    if with_border:
        early = sums.shape[0]
        share = steps // early
        for n in range(steps):
            make_left(start, left_a, n, inner_tiles)
        for p in range(early):
            d = directions_ref[p]
            left, later = lefts[p % 2], lefts[(p + 1) % 2]
            x = product(upper, left, inner_columns, inner_ref[d])
            for n in range(p * share, p * share + share // 2):
                displace(n)
            if p + 1 < early:
                for n in range(steps // 2):
                    make_left(p + 1, later, n, inner_tiles)
            y = product(lower_rows, left, inner_columns, inner_ref[d])
            for n in range(p * share + share // 2, p * share + share):
                displace(n)
            if p + 1 < early:
                for n in range(steps // 2, steps):
                    make_left(p + 1, later, n, inner_tiles)
            sums[p, 0] = x[:, :count] - y[:, count:]
            sums[p, 1] = x[:, count:] + y[:, :count]
        for p in range(early):
            d = directions_ref[p]
            left = lefts[p % 2]
            for n in range(steps):
                make_left(p, left, n, last_tiles)
            x = product(upper, left, last_columns, outer[d])
            y = product(lower_rows, left, last_columns, outer[d])
            write(p, sums[p, 0] + x[:, :count] - y[:, count:], sums[p, 1] + x[:, count:] + y[:, :count])
    begin = start + early
    for n in range(steps if begin < stop else 0):
        make_left(begin, left_a, n, all_tiles)
    for p in range(begin, stop):
        d = directions_ref[p]
        left = lefts[(p - begin) % 2]
        later = lefts[(p + 1 - begin) % 2]
        x = product(upper, left, inner_columns, inner_ref[d]) + product(upper, left, last_columns, outer[d])
        if p + 1 < stop:
            for n in range(steps // 2):
                make_left(p + 1, later, n, all_tiles)
        y = product(lower_rows, left, inner_columns, inner_ref[d]) + product(lower_rows, left, last_columns, outer[d])
        if p + 1 < stop:
            for n in range(steps // 2, steps):
                make_left(p + 1, later, n, all_tiles)
        write(p, x[:, :count] - y[:, count:], x[:, count:] + y[:, :count])


def halve_kernel(following, keep_ref, got_ref, *outs):
    mine = lax.axis_index("gz") // following % 2
    inner_ref, send_ref = outs
    inner_ref[...] = keep_ref[:, :, mine] + got_ref[:, :, mine].astype(F32)
    send_ref[...] = (keep_ref[:, :, 1 - mine] + got_ref[:, :, 1 - mine].astype(F32)).astype(BF16)


def exchange(send, bit):
    return lax.ppermute(send, "gz", [(i, i ^ bit) for i in range(lax.axis_size("gz"))])


def halve(keep, got, following, bits):
    vmem = pl.BlockSpec(memory_space=pltpu.VMEM)
    lead = keep.shape[0] * 2
    rows, columns = keep.shape[2:]
    outer = 2 ** bits.index(following)
    bits.remove(following)
    split = (lead, outer, 2, rows // (2 * outer), columns)
    half = (lead, outer, rows // (2 * outer), columns)
    keep, send = pl.pallas_call(
        functools.partial(halve_kernel, following),
        out_shape=[jax.ShapeDtypeStruct(half, F32), jax.ShapeDtypeStruct(half, BF16)],
        in_specs=[vmem] * 2,
        out_specs=[vmem] * 2,
        compiler_params=pltpu.CompilerParams(vmem_limit_bytes=VMEM_LIMIT),
    )(keep.reshape(split), got.reshape(split))
    shape = (lead // 2, 2, rows // 2, columns)
    return keep.reshape(shape), send.reshape(shape)


def finish_kernel(*refs):
    out_ref = refs[-1]
    at = 0
    for keep_ref, got_ref in zip(refs[0:-1:2], refs[1:-1:2]):
        size = keep_ref.shape[0]
        out_ref[at : at + size] = keep_ref[...] + got_ref[...].astype(F32)
        at += size


def body(eigvecs, gauge_links, momenta, directions):
    device_count = lax.axis_size("gz")
    v = jnp.swapaxes(eigvecs[0], 2, 3)
    u = jnp.transpose(gauge_links[0], (0, 2, 3, 1, 4))
    side = NX // 4
    sites, count = v.shape[2:]
    z_blocks = device_count // 16
    wide = -(-sites // LANES) * LANES
    tiles = wide // LANES
    tail = sites - wide + LANES
    if sites != side * (NY // 4) or device_count & (device_count - 1) or count % device_count:
        raise ValueError("unsupported block")
    if tiles < 3 or tail < 2 * side or tail + 2 * side > LANES:
        raise ValueError("unsupported sites")
    np_ = momenta.shape[0]
    factor = (3.0 * NX * NY * z_blocks) ** (-0.5)
    vmem = pl.BlockSpec(memory_space=pltpu.VMEM)
    smem = pl.BlockSpec(memory_space=pltpu.SMEM)
    params = pltpu.CompilerParams(vmem_limit_bytes=VMEM_LIMIT)
    face = jax.ShapeDtypeStruct((6 * side, count), BF16)
    arguments = [pltpu.with_memory_space_constraint(x, pltpu.HBM) for x in (momenta.T, v, u)]
    near_momenta, near_v, near_u, low_x, low_y, high_y = pl.pallas_call(
        functools.partial(faces_kernel, side),
        out_shape=[jax.ShapeDtypeStruct(x.shape, x.dtype) for x in arguments] + [face] * 3,
        in_specs=[pl.BlockSpec(memory_space=pltpu.HBM)] * 3,
        out_specs=[vmem] * 6,
        scratch_shapes=[
            pltpu.VMEM((count // LANES, sites, LANES), F32),
            pltpu.SemaphoreType.DMA((6,)),
            pltpu.SemaphoreType.DMA((2,)),
        ],
        compiler_params=pltpu.CompilerParams(vmem_limit_bytes=FACES_LIMIT),
        name="faces",
    )(*arguments)

    def sent(face, stride, sign):
        of = side_route(stride, sign)
        return lax.ppermute(face, "gz", [(i, of(i)) for i in range(device_count)])

    halos = [sent(low_x, 4, -1), sent(low_y, 1, -1)]
    applications = 6 if z_blocks > 1 else 5
    operands = [near_momenta, near_v, near_u]
    shapes = [
        jax.ShapeDtypeStruct((6, count, wide), F32),
        jax.ShapeDtypeStruct((2, np_, wide), F32),
        jax.ShapeDtypeStruct((3, 2, np_, LANES), F32),
        jax.ShapeDtypeStruct((applications * 27, 8, wide), F32),
        jax.ShapeDtypeStruct((27, 8, LANES), F32),
    ]
    if z_blocks > 1:
        operands += [
            lax.ppermute(v, "gz", route(device_count, -16)),
            lax.ppermute(v, "gz", route(device_count, 16)),
            lax.ppermute(u[2:3], "gz", route(device_count, 16)),
        ]
        shapes.append(jax.ShapeDtypeStruct((2, 6, count, wide), BF16))
    shapes.append(jax.ShapeDtypeStruct((3, 2 * count, 3 * (tiles - 1) * LANES), BF16))
    results = pl.pallas_call(
        functools.partial(interior_kernel, side, z_blocks),
        out_shape=shapes,
        in_specs=[vmem] * len(operands),
        out_specs=[vmem] * len(shapes),
        scratch_shapes=[pltpu.VMEM((4, 6, 16, wide), F32)],
        compiler_params=params,
        name="interior",
    )(*operands)
    vp, tab, last_tab, coef, side_coef = results[:5]
    inner = results[-1]
    vz = list(results[5:-1])
    half = count // 2
    per = count // device_count
    lead = (device_count // 2, per, count)

    def products(start, stop, extra, table, done=()):
        with_border = not start
        extra = [*extra, *done]
        size = stop - start + (done[0].shape[0] if done else 0)
        operands = [directions, vp, table, last_tab, inner, *extra]
        shapes = [
            jax.ShapeDtypeStruct((size, 2) + lead, F32),
            jax.ShapeDtypeStruct((size, 2) + lead, BF16),
        ]
        scratch = [
            pltpu.VMEM((2 * count, 3 * wide), BF16),
            pltpu.VMEM((2 * count, 3 * wide), BF16),
            pltpu.VMEM((2, device_count // 2, 2, per, count), F32),
        ]
        if with_border:
            shapes.append(jax.ShapeDtypeStruct((3, 2 * count, 3 * LANES), BF16))
            shapes.append(jax.ShapeDtypeStruct((3, 6, count, LANES), F32))
            scratch.append(pltpu.VMEM((6, count, LANES), F32))
            early = max(n for n in (1, 2, 4) if n <= stop and count // 16 % (2 * n) == 0)
            scratch.append(pltpu.VMEM((early, 2, count, count), F32))
        results = pl.pallas_call(
            functools.partial(products_kernel, side, sites, z_blocks, factor, start, stop, with_border),
            out_shape=shapes,
            in_specs=[smem] + [vmem] * (len(operands) - 1),
            out_specs=[vmem] * len(shapes),
            scratch_shapes=scratch,
            compiler_params=params,
        )(*operands)
        return results[0], results[1], results[2:]

    def flat(x):
        return x.reshape(x.shape[:2] + (half, count))

    order = [2**n for n in range(device_count.bit_length() - 1)]
    other = [order[0], order[2], order[1]] + order[3:]
    cut, between = np_ * CUTS[0] // 8, np_ * CUTS[1] // 8
    bits_a, bits_b = order[:0:-1], order[:0:-1]
    keep_a, send_a, behind = products(0, cut, [coef, side_coef, high_y, *halos, *vz], tab)
    keep_a = flat(keep_a)
    got_a = exchange(flat(send_a), order[0])
    done = products(cut, between, behind, tab)[:2]
    got_a, send_b = lax.optimization_barrier((got_a, done[1]))
    keep_a, send_a = halve(keep_a, got_a, order[1], bits_a)
    send_a, table = lax.optimization_barrier((send_a, tab))
    got_a = exchange(send_a, order[1])
    keep_b, send_b, _ = products(between, np_, behind, table, (done[0], send_b))
    keep_b = flat(keep_b)
    got_b = exchange(flat(send_b), other[0])
    for n in range(1, len(order)):
        keep_b, send_b = halve(keep_b, got_b, other[n], bits_b)
        got_b = exchange(send_b, other[n])
        if n + 1 < len(order):
            keep_a, send_a = halve(keep_a, got_a, order[n + 1], bits_a)
            got_a = exchange(send_a, order[n + 1])
    return pl.pallas_call(
        finish_kernel,
        out_shape=jax.ShapeDtypeStruct((np_,) + keep_a.shape[1:], F32),
        in_specs=[vmem] * 4,
        out_specs=vmem,
        compiler_params=params,
        name="finish",
    )(keep_a, got_a, keep_b, got_b)


def solution(mesh):
    return jax.shard_map(
        body,
        mesh=mesh,
        in_specs=(
            P(("slab", "gz"), None, None, None, None),
            P(("slab", "gz"), None, None, None, None, None),
            P(),
            P(),
        ),
        out_specs=P("slab", None, "gz", None),
        check_vma=False,
    )
```
